32 devices in a mesh: img: 2 (over y), row: 4 (over x, core), col: 4 (over z).
Axes of the slice: x: 2, y: 2, z: 4, core: 2. Of those that a mesh axis runs over, the one named last changes fastest.
Arguments:
- tokens: bfloat16 [4112, 1024], P(('img', 'row'), 'col'), may hold values from -6 to 6
- attn_bias: bfloat16 [16, 257, 257], P('col'), may hold values from -5 to 250
- first_gain: float32 [1024], P('col'), may hold values from 0.5 to 1.5
- first_shift: float32 [1024], P('col'), may hold values from -3 to 3
- qkv_weight: bfloat16 [1024, 3, 1024], P('row', None, 'col'), may hold values from -0.1875 to 0.1875
- qkv_bias: float32 [2, 1024], P(None, 'col'), may hold values from -3 to 3
- proj_weight: bfloat16 [1024, 1024], P('row', 'col'), may hold values from -0.75 to 0.75
- proj_bias: float32 [1024], P('col'), may hold values from -3 to 3
- scale_attn: float32 [1024], P('col'), may hold values from 0.5 to 2
- second_gain: float32 [1024], P('col'), may hold values from 0.5 to 1.5
- second_shift: float32 [1024], P('col'), may hold values from -3 to 3
- fc1_weight: bfloat16 [1024, 4096], P('row', 'col'), may hold values from -0.1875 to 0.1875
- fc1_bias: float32 [4096], P('col'), may hold values from -3 to 3
- fc2_weight: bfloat16 [1024, 4096], P('row', 'col'), may hold values from -0.09375 to 0.09375
- fc2_bias: float32 [1024], P('col'), may hold values from -3 to 3
- scale_mlp: float32 [1024], P('col'), may hold values from 0.5 to 2
- cotangent: float32 [4112, 1024], P(('img', 'row'), 'col'), may hold values from -6 to 6
Outputs:
- out_y: float32 [4112, 1024], P(('img', 'row'), 'col')
- grad_tokens: float32 [4112, 1024], P(('img', 'row'), 'col')
- grad_qkv_weight: float32 [1024, 3, 1024], P('row', None, 'col')
- grad_qkv_bias: float32 [2, 1024], P(None, 'col')
- grad_proj_weight: float32 [1024, 1024], P('row', 'col')
- grad_proj_bias: float32 [1024], P('col')
- grad_scale_attn: float32 [1024], P('col')
- grad_fc1_weight: float32 [1024, 4096], P('row', 'col')
- grad_fc1_bias: float32 [4096], P('col')
- grad_fc2_weight: float32 [1024, 4096], P('row', 'col')
- grad_fc2_bias: float32 [1024], P('col')
- grad_scale_mlp: float32 [1024], P('col')
- grad_first_gain: float32 [1024], P('col')
- grad_first_shift: float32 [1024], P('col')
- grad_second_gain: float32 [1024], P('col')
- grad_second_shift: float32 [1024], P('col')
The draws below stay inside these ranges and needn't reach their ends.
All inputs are finite; a program needn't handle non-finite values.
Results may differ from the reference program's by a relative error of at most 0.019.
Values may be sent and summed in bfloat16 or wider, within the bound.
No kernel may reach another device: no remote copies, remote signals or barrier semaphores. Data moves between devices by JAX's collectives and lax.ppermute only.
A program may use at most 128 MiB of HBM per device.

```python
import math
import jax
import jax.numpy as jnp
from jax import lax

HEADS = 16
HEAD_DIM = 64
FF = 4096
D = 1024
SEQ = 257
IMG_DEV = 2
BLOCKS = 4
IMAGES = 16
TOKENS = 4112


def draw_attn_bias(key, part):
    base_key = jax.random.fold_in(key, 11)
    shape = (HEADS, SEQ, SEQ)
    values_table = jnp.clip(jax.random.normal(base_key, shape, jnp.float32), -5.0, 5.0)
    return values_table.astype(jnp.bfloat16)


def shard_levels(own_key, extent, cuts, smallest, largest):
    level = 1.0
    for dim, blocks in cuts:
        steps = jax.random.uniform(jax.random.fold_in(jax.random.fold_in(own_key, 6), dim), (blocks,), jnp.float32, smallest / len(cuts), largest / len(cuts))
        level = level * jnp.repeat(jnp.exp(steps), extent[dim] // blocks).reshape((-1,) + (1,) * (len(extent) - 1 - dim))
    return level


def noise(own_key, shape, spread, limit, cuts=(), kind=jnp.bfloat16):
    values = jax.random.normal(own_key, shape, jnp.float32) * spread
    if len(cuts) > 0:
        values = shard_levels(own_key, shape, cuts, -0.22, 0.18) * values
    return jnp.clip(values, min=-limit, max=limit).astype(kind)


def setup_inputs(seed: int = 0) -> dict:
    key_of = jax.random.split(jax.random.key(seed), 18)
    return {
        "tokens": noise(key_of[0], (TOKENS, D), 1.0, 6.0, ((0, 8), (1, 4))),
        "attn_bias": draw_attn_bias(jax.random.fold_in(key_of[17], 71), 0),
        "first_gain": jnp.clip(1.0 + 0.1 * jax.random.normal(key_of[2], (D,), jnp.float32), 0.5, 1.5),
        "first_shift": noise(key_of[3], (D,), 0.5, 3.0, ((0, 4),), jnp.float32),
        "qkv_weight": noise(key_of[4], (D, 3, D), D ** -0.5, 0.1875, ((0, 4), (2, 4))),
        "qkv_bias": noise(key_of[5], (2, D), 0.5, 3.0, ((1, 4),), jnp.float32),
        "proj_weight": noise(key_of[6], (D, D), (D // 16) ** -0.5, 0.75, ((0, 4), (1, 4))),
        "proj_bias": noise(key_of[7], (D,), 0.5, 3.0, ((0, 4),), jnp.float32),
        "scale_attn": jnp.clip(jnp.exp(math.log(2.0) - 1.3862944 * jax.random.uniform(key_of[8], (D,), jnp.float32) ** shard_levels(key_of[8], (D,), ((0, 4),), -0.2, 0.2)), 0.5, 2.0),
        "second_gain": jnp.clip(1.0 + 0.1 * jax.random.normal(key_of[9], (D,), jnp.float32), 0.5, 1.5),
        "second_shift": noise(key_of[10], (D,), 0.5, 3.0, ((0, 4),), jnp.float32),
        "fc1_weight": noise(key_of[11], (D, FF), D ** -0.5, 0.1875, ((0, 4), (1, 4))),
        "fc1_bias": noise(key_of[12], (FF,), 0.5, 3.0, ((0, 4),), jnp.float32),
        "fc2_weight": noise(key_of[13], (D, FF), FF ** -0.5, 0.09375, ((0, 4), (1, 4))),
        "fc2_bias": noise(key_of[14], (D,), 0.5, 3.0, ((0, 4),), jnp.float32),
        "scale_mlp": jnp.clip(jnp.exp(math.log(2.0) - 1.3862944 * jax.random.uniform(key_of[15], (D,), jnp.float32) ** shard_levels(key_of[15], (D,), ((0, 4),), -0.2, 0.2)), 0.5, 2.0),
        "cotangent": noise(key_of[16], (TOKENS, D), 1.0, 6.0, ((0, 8), (1, 4)), jnp.float32),
    }


EPS = 1e-06
SQRT_HALF = 0.7071067811865476
INV_ROOT_TWO_PI = 0.3989422804014327

def norm_rows(values, gain, shift):
    row_mean = lax.optimization_barrier(jnp.mean(values, axis=-1, keepdims=True))
    row_var = lax.optimization_barrier(jnp.mean(values * values, axis=-1, keepdims=True)) - row_mean * row_mean
    inv_std = lax.rsqrt(row_var + EPS)
    x_hat = (values - row_mean) * inv_std
    return (x_hat, inv_std, (x_hat * gain + shift).astype(jnp.bfloat16))

def norm_back(grad_in, x_hat, inv_std, gain):
    scaled = grad_in * gain
    mean_one = lax.optimization_barrier(jnp.mean(scaled, axis=-1, keepdims=True))
    mean_two = lax.optimization_barrier(jnp.mean(scaled * x_hat, axis=-1, keepdims=True))
    return inv_std * (scaled - mean_one - x_hat * mean_two)

def rounded(values):
    return lax.optimization_barrier(values.astype(jnp.bfloat16)).astype(jnp.float32)

def block_sums(left, right):
    count_rows = left.shape[0]
    width = left.shape[-1]
    middle = left.shape[1:-1]
    left_blocks = left.astype(jnp.float32).reshape((count_rows,) + middle + (BLOCKS, width // BLOCKS))
    right_blocks = right.astype(jnp.float32).reshape((right.shape[0],) + middle + (BLOCKS, width // BLOCKS))
    if len(middle) == 0:
        pattern = 'rcf,ocf->cro'
    else:
        pattern = 'rjcf,ojcf->cro'
    parts = jnp.einsum(pattern, left_blocks, right_blocks)
    return lax.optimization_barrier(jnp.sum(rounded(parts), axis=0))

def gelu_value(pre_act):
    return 0.5 * pre_act * (1.0 + lax.erf(pre_act * SQRT_HALF))

def gelu_slope(pre_act):
    return 0.5 * (1.0 + lax.erf(pre_act * SQRT_HALF)) + pre_act * jnp.exp(-0.5 * pre_act * pre_act) * INV_ROOT_TWO_PI

def split_heads(heads_in, images, head_count):
    head_grid = heads_in.astype(jnp.float32).reshape(images, SEQ, 3, head_count, HEAD_DIM)
    return (head_grid[:, :, 0], head_grid[:, :, 1], head_grid[:, :, 2])

def score_block(query_heads, key_heads, bias_f, score_scale):
    return jnp.einsum('gqhe,gkhe->ghqk', query_heads, key_heads) * score_scale + bias_f

def attend(heads_in, bias_f, images, head_count, score_scale):
    query_heads, key_heads, value_heads = split_heads(heads_in, images, head_count)
    scores = score_block(query_heads, key_heads, bias_f, score_scale)
    row_max = lax.optimization_barrier(jnp.max(scores, axis=-1, keepdims=True))
    log_total = row_max + jnp.log(lax.optimization_barrier(jnp.sum(jnp.exp(scores - row_max), axis=-1, keepdims=True)))
    weights_half = rounded(jnp.exp(scores - log_total))
    output = jnp.einsum('ghqk,gkhe->gqhe', weights_half, value_heads)
    return (output.reshape(images * SEQ, head_count * HEAD_DIM).astype(jnp.bfloat16), log_total)

def attend_back(heads_in, bias_f, log_total, grad_heads, images, head_count, score_scale):
    query_heads, key_heads, value_heads = split_heads(heads_in, images, head_count)
    scores = score_block(query_heads, key_heads, bias_f, score_scale)
    prob_full = jnp.exp(scores - log_total)
    prob_half = rounded(prob_full)
    grad_out = grad_heads.astype(jnp.float32).reshape(images, SEQ, head_count, HEAD_DIM)
    grad_value = jnp.einsum('ghqk,gqhe->gkhe', prob_half, grad_out)
    grad_prob = jnp.einsum('gqhe,gkhe->ghqk', grad_out, value_heads)
    row_dot = lax.optimization_barrier(jnp.sum(prob_full * grad_prob, axis=-1, keepdims=True))
    grad_s = rounded(prob_full * (grad_prob - row_dot))
    grad_query = jnp.einsum('ghqk,gkhe->gqhe', grad_s, key_heads) * score_scale
    grad_key = jnp.einsum('ghqk,gqhe->gkhe', grad_s, query_heads) * score_scale
    flat_shape = (images * SEQ, head_count * HEAD_DIM)
    stacked = jnp.stack([grad_query.reshape(flat_shape), grad_key.reshape(flat_shape), grad_value.reshape(flat_shape)], axis=1)
    return stacked.astype(jnp.bfloat16)

def add_pairs(left, right):
    return left + right

def reference(tokens, attn_bias, first_gain, first_shift, qkv_weight, qkv_bias, proj_weight, proj_bias, scale_attn, second_gain, second_shift, fc1_weight, fc1_bias, fc2_weight, fc2_bias, scale_mlp, cotangent):
    groups = IMAGES // IMG_DEV
    count_rows = IMG_DEV * SEQ
    bias_f = attn_bias.astype(jnp.float32)[None]
    score_scale = HEAD_DIM ** (-0.5)
    qkv_flat = qkv_weight.reshape(D, 3 * D)

    def one_group(totals, inputs):
        x_in, grad_y = inputs
        x_val = x_in.astype(jnp.float32)
        hat_first, inv_first, first_norm = norm_rows(x_val, first_gain, first_shift)
        mixed_all = jnp.dot(first_norm, qkv_flat, preferred_element_type=jnp.float32).reshape(count_rows, 3, D)
        heads_in = jnp.stack([mixed_all[:, 0] + qkv_bias[0], mixed_all[:, 1], mixed_all[:, 2] + qkv_bias[1]], axis=1).astype(jnp.bfloat16)
        attn_out, log_total = attend(heads_in, bias_f, IMG_DEV, HEADS, score_scale)
        proj_val = block_sums(attn_out, proj_weight) + proj_bias
        x_mid = x_val + scale_attn * proj_val
        hat_second, inv_second, second_norm = norm_rows(x_mid, second_gain, second_shift)
        pre_act = jnp.dot(second_norm, fc1_weight, preferred_element_type=jnp.float32) + fc1_bias
        act_val = gelu_value(pre_act).astype(jnp.bfloat16)
        mlp_val = block_sums(act_val, fc2_weight) + fc2_bias
        out_y = x_mid + scale_mlp * mlp_val
        grad_mlp = (grad_y * scale_mlp).astype(jnp.bfloat16)
        grad_act = jnp.dot(grad_mlp, fc2_weight, preferred_element_type=jnp.float32)
        grad_pre = (grad_act * gelu_slope(pre_act)).astype(jnp.bfloat16)
        grad_two = block_sums(grad_pre, fc1_weight)
        grad_mid = grad_y + norm_back(grad_two, hat_second, inv_second, second_gain)
        grad_attn_in = (grad_mid * scale_attn).astype(jnp.bfloat16)
        grad_heads = jnp.dot(grad_attn_in, proj_weight, preferred_element_type=jnp.float32).astype(jnp.bfloat16)
        grad_qkv = attend_back(heads_in, bias_f, log_total, grad_heads, IMG_DEV, HEADS, score_scale)
        grad_one = block_sums(grad_qkv, qkv_weight)
        grad_x = grad_mid + norm_back(grad_one, hat_first, inv_first, first_gain)
        grad_qkv_f = grad_qkv.astype(jnp.float32)
        grad_terms = (jnp.dot(first_norm.T, grad_qkv.reshape(count_rows, 3 * D), preferred_element_type=jnp.float32).reshape(D, 3, D), jnp.stack([lax.optimization_barrier(jnp.sum(grad_qkv_f[:, 0], axis=0)), lax.optimization_barrier(jnp.sum(grad_qkv_f[:, 2], axis=0))], axis=0), jnp.dot(grad_attn_in.T, attn_out, preferred_element_type=jnp.float32), lax.optimization_barrier(jnp.sum(grad_mid * scale_attn, axis=0)), lax.optimization_barrier(jnp.sum(grad_mid * proj_val, axis=0)), jnp.dot(second_norm.T, grad_pre, preferred_element_type=jnp.float32), lax.optimization_barrier(jnp.sum(grad_pre.astype(jnp.float32), axis=0)), jnp.dot(grad_mlp.T, act_val, preferred_element_type=jnp.float32), lax.optimization_barrier(jnp.sum(grad_y * scale_mlp, axis=0)), lax.optimization_barrier(jnp.sum(grad_y * mlp_val, axis=0)), lax.optimization_barrier(jnp.sum(grad_one * hat_first, axis=0)), lax.optimization_barrier(jnp.sum(grad_one, axis=0)), lax.optimization_barrier(jnp.sum(grad_two * hat_second, axis=0)), lax.optimization_barrier(jnp.sum(grad_two, axis=0)))
        return (jax.tree.map(add_pairs, totals, grad_terms), (out_y, grad_x))
    start_totals = (jnp.zeros((D, 3, D), jnp.float32), jnp.zeros((2, D), jnp.float32), jnp.zeros((D, D), jnp.float32), jnp.zeros((D,), jnp.float32), jnp.zeros((D,), jnp.float32), jnp.zeros((D, FF), jnp.float32), jnp.zeros((FF,), jnp.float32), jnp.zeros((D, FF), jnp.float32), jnp.zeros((D,), jnp.float32), jnp.zeros((D,), jnp.float32), jnp.zeros((D,), jnp.float32), jnp.zeros((D,), jnp.float32), jnp.zeros((D,), jnp.float32), jnp.zeros((D,), jnp.float32))
    inputs = (tokens.reshape(groups, count_rows, D), cotangent.reshape(groups, count_rows, D))
    totals, outputs = lax.scan(one_group, start_totals, inputs)
    out_y = outputs[0].reshape(TOKENS, D)
    grad_tokens = outputs[1].reshape(TOKENS, D)
    return (out_y, grad_tokens, totals[0], totals[1], totals[2], totals[3], totals[4], totals[5], totals[6], totals[7], totals[8], totals[9], totals[10], totals[11], totals[12], totals[13])
```

```python
import jax
import jax.numpy as jnp
from jax import lax
from jax.sharding import PartitionSpec as P

HEAD_DIM = 64
SEQ = 257
EPS = 1e-06
SQRT_HALF = 0.7071067811865476
INV_ROOT_TWO_PI = 0.3989422804014327

BF = jnp.bfloat16
F32 = jnp.float32


def dot(left, right, dims):
    return lax.dot_general(left, right, (dims, ((), ())), preferred_element_type=F32)


def bits_of(count):
    out = []
    bit = 1
    while bit < count:
        out.append(bit)
        bit *= 2
    return out


def make_body(n_img, n_row, n_col):
    sizes = {"img": n_img, "row": n_row, "col": n_col}

    def swap(value, axis, mask):
        return lax.ppermute(value, axis, [(i, i ^ mask) for i in range(sizes[axis])])

    def reorder(pieces, axis):
        index = lax.axis_index(axis)
        for bit in bits_of(sizes[axis]):
            flag = (index & bit) != 0
            pieces = [
                jnp.where(flag, pieces[k ^ bit], pieces[k]) for k in range(len(pieces))
            ]
        return pieces

    def spread(value, axis):
        pieces = [value] * sizes[axis]
        for k in range(1, sizes[axis]):
            low = k & -k
            pieces[k] = swap(pieces[k ^ low], axis, low)
        return pieces

    def gather_blocks(value):
        return reorder(spread(value, "col"), "col")

    def direct_sum(value, axis):
        total = value
        for k in range(1, sizes[axis]):
            total = total + swap(value, axis, k)
        return total

    def scatter_cols(full):
        width = full.shape[1] // n_col
        half = full.astype(BF)
        blocks = [half[:, k * width : (k + 1) * width] for k in range(n_col)]
        mine = reorder(blocks, "col")
        total = mine[0].astype(F32)
        for k in range(1, n_col):
            total = total + swap(mine[k], "col", k).astype(F32)
        return total

    def all_sum(value, axes):
        for axis in axes:
            for bit in bits_of(sizes[axis]):
                value = value + swap(value, axis, bit)
        return value

    def gather_rows(value):
        index = lax.axis_index("row")
        lead, rows, width = value.shape
        pieces = [value] * n_row
        for bit in reversed(bits_of(n_row)):
            for k in range(0, n_row, 2 * bit):
                pieces[k ^ bit] = swap(pieces[k], "row", bit)
        full = jnp.zeros((lead, n_row, rows, width), value.dtype)
        for k in range(n_row):
            full = lax.dynamic_update_slice(full, pieces[k][:, None], (0, index ^ k, 0, 0))
        return full.reshape(lead, n_row * rows, width)

    def reduce_weight(grad):
        index = lax.axis_index("row")
        lead, total_rows, width = grad.shape
        rows = total_rows // n_row
        parts = grad.astype(BF).reshape(lead, n_row, rows, width)
        for bit in bits_of(n_row):
            count = parts.shape[1]
            pairs = parts.reshape(lead, count // 2, 2, rows, width)
            flag = (index & bit) != 0
            keep = jnp.where(flag, pairs[:, :, 1], pairs[:, :, 0])
            send = jnp.where(flag, pairs[:, :, 0], pairs[:, :, 1])
            parts = (keep.astype(F32) + swap(send, "row", bit).astype(F32)).astype(BF)
        share = parts[:, 0]
        for bit in bits_of(n_img):
            share = (share.astype(F32) + swap(share, "img", bit).astype(F32))
            if bit * 2 < n_img:
                share = share.astype(BF)
        return share.astype(F32)

    def body(
        tokens,
        attn_bias,
        first_gain,
        first_shift,
        qkv_weight,
        qkv_bias,
        proj_weight,
        proj_bias,
        scale_attn,
        second_gain,
        second_shift,
        fc1_weight,
        fc1_bias,
        fc2_weight,
        fc2_bias,
        scale_mlp,
        cotangent,
    ):
        count_rows, width = tokens.shape
        images = range(count_rows // SEQ)
        model = width * n_col
        head_count = qkv_weight.shape[2] // HEAD_DIM
        score_scale = HEAD_DIM ** (-0.5)
        bias_f = attn_bias.astype(F32)
        col = lax.axis_index("col")

        x_in = [tokens[g * SEQ : (g + 1) * SEQ] for g in images]
        cot = [cotangent[g * SEQ : (g + 1) * SEQ] for g in images]

        vectors = jnp.stack([first_gain, first_shift, second_gain, second_shift], axis=0)
        vec_full = jnp.concatenate(gather_blocks(vectors), axis=1)
        gain_one, shift_one, gain_two, shift_two = (vec_full[k][None] for k in range(4))

        x_blocks = [gather_blocks(x_in[g]) for g in images]
        w_qkv = gather_rows(jnp.transpose(qkv_weight, (1, 0, 2)))
        w_proj = gather_rows(proj_weight[None])[0]
        w_fc1 = gather_rows(fc1_weight[None])[0]
        w_fc2 = gather_rows(fc2_weight[None])[0]
        grad_mlp = [
            jnp.concatenate(gather_blocks((cot[g] * scale_mlp).astype(BF)), axis=1) for g in images
        ]

        hat_one, inv_one, norm_one = [], [], []
        q_in, k_in, v_in = [], [], []
        attn_out, log_total = [], []
        x_val = [v.astype(F32) for v in x_in]
        x_mid, proj_val, hat_two, inv_two, norm_two, hat_two_own = [], [], [], [], [], []
        for g in images:
            full = jnp.concatenate(x_blocks[g], axis=1).astype(F32)
            mean = jnp.mean(full, axis=1, keepdims=True)
            var = jnp.mean(full * full, axis=1, keepdims=True) - mean * mean
            inv = lax.rsqrt(var + EPS)
            hat = (full - mean) * inv
            hat_one.append(hat)
            inv_one.append((mean, inv))
            norm = (hat * gain_one + shift_one).astype(BF)
            norm_one.append(norm)
            q_in.append((dot(norm, w_qkv[0], ((1,), (0,))) + qkv_bias[0]).astype(BF))
            k_in.append(dot(norm, w_qkv[1], ((1,), (0,))).astype(BF))
            v_in.append((dot(norm, w_qkv[2], ((1,), (0,))) + qkv_bias[1]).astype(BF))
            heads = lambda a: a.reshape(SEQ, head_count, HEAD_DIM)
            scores = (
                jnp.einsum("qhe,khe->hqk", heads(q_in[g]), heads(k_in[g]), preferred_element_type=F32)
                * score_scale
                + bias_f
            )
            row_max = jnp.max(scores, axis=-1, keepdims=True)
            log_sum = row_max + jnp.log(jnp.sum(jnp.exp(scores - row_max), axis=-1, keepdims=True))
            log_total.append(log_sum)
            weights_half = jnp.exp(scores - log_sum).astype(BF)
            out = jnp.einsum("hqk,khe->qhe", weights_half, heads(v_in[g]), preferred_element_type=F32)
            attn_out.append(out.reshape(SEQ, head_count * HEAD_DIM).astype(BF))

            proj_val.append(scatter_cols(dot(attn_out[g], w_proj, ((1,), (1,)))) + proj_bias)
            x_mid.append(x_val[g] + scale_attn * proj_val[g])
            mean_own = jnp.mean(x_mid[g], axis=1)
            centred = x_mid[g] - mean_own[:, None]
            var_own = jnp.mean(centred * centred, axis=1)
            sent = (centred * lax.rsqrt(var_own + EPS)[:, None]).astype(BF)
            stats = spread(jnp.stack([mean_own, var_own], axis=0), "col")
            mean = sum(s[0] for s in stats) / n_col
            var = sum(s[1] + (s[0] - mean) * (s[0] - mean) for s in stats) / n_col
            inv = lax.rsqrt(var + EPS)
            got = spread(sent, "col")
            hats = [
                got[k].astype(F32) * (jnp.sqrt(stats[k][1] + EPS) * inv)[:, None]
                + ((stats[k][0] - mean) * inv)[:, None]
                for k in range(n_col)
            ]
            inv_two.append(inv)
            hat_two_own.append((x_mid[g] - mean[:, None]) * inv[:, None])
            hat = jnp.concatenate(reorder([h.astype(BF) for h in hats], "col"), axis=1)
            hat_two.append(hat)
            norm_two.append((hat.astype(F32) * gain_two + shift_two).astype(BF))

        grad_pre, act_val, grad_two, grad_mid, grad_attn_in = [], [], [], [], []
        for g in images:
            pre = dot(norm_two[g], w_fc1, ((1,), (0,))) + fc1_bias
            gate = 0.5 * (1.0 + lax.erf(pre * SQRT_HALF))
            act_val.append((pre * gate).astype(BF))
            slope = gate + pre * jnp.exp(-0.5 * pre * pre) * INV_ROOT_TWO_PI
            grad_act = dot(grad_mlp[g], w_fc2, ((1,), (0,)))
            grad_pre.append((grad_act * slope).astype(BF))
            part = dot(grad_pre[g], w_fc1, ((1,), (1,)))
            scaled = part * gain_two
            totals = direct_sum(
                jnp.stack(
                    [jnp.sum(scaled, axis=1), jnp.sum(scaled * hat_two[g].astype(F32), axis=1)], axis=0
                ),
                "col",
            ) / model
            grad_two.append(scatter_cols(part))
            grad_mid.append(
                cot[g]
                + inv_two[g][:, None]
                * (
                    grad_two[g] * second_gain
                    - totals[0][:, None]
                    - hat_two_own[g] * totals[1][:, None]
                )
            )
            grad_attn_in.append(
                jnp.concatenate(gather_blocks((grad_mid[g] * scale_attn).astype(BF)), axis=1)
            )

        grad_q, grad_k, grad_v, grad_one, grad_tokens, hat_one_own = [], [], [], [], [], []
        for g in images:
            grad_heads = dot(grad_attn_in[g], w_proj, ((1,), (0,))).astype(BF)
            heads = lambda a: a.reshape(SEQ, head_count, HEAD_DIM)
            scores = (
                jnp.einsum("qhe,khe->hqk", heads(q_in[g]), heads(k_in[g]), preferred_element_type=F32)
                * score_scale
                + bias_f
            )
            prob = jnp.exp(scores - log_total[g])
            prob_half = prob.astype(BF)
            d_v = jnp.einsum("hqk,qhe->khe", prob_half, heads(grad_heads), preferred_element_type=F32)
            d_p = jnp.einsum(
                "qhe,khe->hqk", heads(grad_heads), heads(v_in[g]), preferred_element_type=F32
            )
            row_dot = jnp.sum(prob * d_p, axis=-1, keepdims=True)
            d_s = (prob * (d_p - row_dot)).astype(BF)
            d_q = jnp.einsum("hqk,khe->qhe", d_s, heads(k_in[g]), preferred_element_type=F32)
            d_k = jnp.einsum("hqk,qhe->khe", d_s, heads(q_in[g]), preferred_element_type=F32)
            flat = lambda a: a.reshape(SEQ, head_count * HEAD_DIM).astype(BF)
            grad_q.append(flat(d_q * score_scale))
            grad_k.append(flat(d_k * score_scale))
            grad_v.append(flat(d_v))
            part = (
                dot(grad_q[g], w_qkv[0], ((1,), (1,)))
                + dot(grad_k[g], w_qkv[1], ((1,), (1,)))
                + dot(grad_v[g], w_qkv[2], ((1,), (1,)))
            )
            scaled = part * gain_one
            totals = direct_sum(
                jnp.stack([jnp.sum(scaled, axis=1), jnp.sum(scaled * hat_one[g], axis=1)], axis=0),
                "col",
            ) / model
            grad_one.append(scatter_cols(part))
            mean, inv = inv_one[g]
            hat_one_own.append((x_val[g] - mean) * inv)
            grad_tokens.append(
                grad_mid[g]
                + inv
                * (
                    grad_one[g] * first_gain
                    - totals[0][:, None]
                    - hat_one_own[g] * totals[1][:, None]
                )
            )

        def over_tokens(left, right):
            return sum(dot(left[g], right[g], ((0,), (0,))) for g in images)

        grad_fc2 = reduce_weight(over_tokens(grad_mlp, act_val)[None])[0]
        grad_fc1 = reduce_weight(over_tokens(norm_two, grad_pre)[None])[0]
        grad_proj = reduce_weight(over_tokens(grad_attn_in, attn_out)[None])[0]
        grad_qkv = reduce_weight(
            jnp.stack([over_tokens(norm_one, d) for d in (grad_q, grad_k, grad_v)], axis=0)
        )

        mlp_val = [scatter_cols(dot(act_val[g], w_fc2, ((1,), (1,)))) + fc2_bias for g in images]
        out_y = [x_mid[g] + scale_mlp * mlp_val[g] for g in images]

        def token_sum(terms):
            return sum(jnp.sum(t.astype(F32), axis=0) for t in terms)

        sums = [
            token_sum(grad_q),
            token_sum(grad_v),
            token_sum([grad_mid[g] * scale_attn for g in images]),
            token_sum([grad_mid[g] * proj_val[g] for g in images]),
            token_sum([cot[g] * scale_mlp for g in images]),
            token_sum([cot[g] * mlp_val[g] for g in images]),
            token_sum([grad_one[g] * hat_one_own[g] for g in images]),
            token_sum(grad_one),
            token_sum([grad_two[g] * hat_two_own[g] for g in images]),
            token_sum(grad_two),
        ]
        sums = all_sum(jnp.stack(sums, axis=0), ("row", "img"))
        sum_pre = all_sum(token_sum(grad_pre), ("row", "img"))
        return (
            jnp.concatenate(out_y, axis=0),
            jnp.concatenate(grad_tokens, axis=0),
            jnp.transpose(grad_qkv, (1, 0, 2)),
            sums[:2],
            grad_proj,
            sums[2],
            sums[3],
            grad_fc1,
            sum_pre,
            grad_fc2,
            sums[4],
            sums[5],
            sums[6],
            sums[7],
            sums[8],
            sums[9],
        )

    return body


def solution(mesh):
    return jax.shard_map(
        make_body(mesh.shape["img"], mesh.shape["row"], mesh.shape["col"]),
        mesh=mesh,
        in_specs=(
            P(("img", "row"), "col"),
            P("col", None, None),
            P("col"),
            P("col"),
            P("row", None, "col"),
            P(None, "col"),
            P("row", "col"),
            P("col"),
            P("col"),
            P("col"),
            P("col"),
            P("row", "col"),
            P("col"),
            P("row", "col"),
            P("col"),
            P("col"),
            P(("img", "row"), "col"),
        ),
        out_specs=(
            P(("img", "row"), "col"),
            P(("img", "row"), "col"),
            P("row", None, "col"),
            P(None, "col"),
            P("row", "col"),
            P("col"),
            P("col"),
            P("row", "col"),
            P("col"),
            P("row", "col"),
            P("col"),
            P("col"),
            P("col"),
            P("col"),
            P("col"),
            P("col"),
        ),
        check_vma=False,
    )
```

```python
import jax
import jax.numpy as jnp
from jax import lax
from jax.sharding import PartitionSpec as P

HEAD_DIM = 64
SEQ = 257
EPS = 1e-06
SQRT_HALF = 0.7071067811865476
INV_ROOT_TWO_PI = 0.3989422804014327

BF = jnp.bfloat16
F32 = jnp.float32


def dot(left, right, dims):
    return lax.dot_general(left, right, (dims, ((), ())), preferred_element_type=F32)


def bits_of(count):
    out = []
    bit = 1
    while bit < count:
        out.append(bit)
        bit *= 2
    return out


def make_body(n_img, n_row, n_col):
    sizes = {"img": n_img, "row": n_row, "col": n_col}

    def swap(value, axis, mask):
        return lax.ppermute(value, axis, [(i, i ^ mask) for i in range(sizes[axis])])

    def tree_order(axis):
        order = [0]
        for bit in reversed(bits_of(sizes[axis])):
            order = order + [m | bit for m in order]
        return order

    def reorder(pieces, axis):
        index = lax.axis_index(axis)
        for bit in bits_of(sizes[axis]):
            flag = (index & bit) != 0
            pieces = [
                jnp.where(flag, pieces[k ^ bit], pieces[k]) for k in range(len(pieces))
            ]
        return pieces

    def gather_blocks(value):
        held = value[None]
        for bit in reversed(bits_of(n_col)):
            held = jnp.concatenate([held, swap(held, "col", bit)], axis=0)
        order = tree_order("col")
        return reorder([held[order.index(k)] for k in range(n_col)], "col")

    def gather_cols(value):
        return jnp.concatenate(gather_blocks(value), axis=-1)

    def tree_scatter(blocks, axis, last=F32):
        held = jnp.stack([blocks[m] for m in tree_order(axis)], axis=0)
        bits = bits_of(sizes[axis])
        for bit in bits:
            half = held.shape[0] // 2
            got = swap(held[half:], axis, bit)
            held = held[:half].astype(F32) + got.astype(F32)
            held = held.astype(last if bit == bits[-1] else BF)
        return held[0]

    def scatter_cols(full):
        width = full.shape[-1] // n_col
        half = full.astype(BF)
        blocks = [half[..., k * width : (k + 1) * width] for k in range(n_col)]
        return tree_scatter(reorder(blocks, "col"), "col")

    def all_sum(value, axes):
        for axis in axes:
            for bit in bits_of(sizes[axis]):
                value = value + swap(value, axis, bit)
        return value

    def gather_rows(values):
        index = lax.axis_index("row")
        rows, width = values[0].shape
        pieces = [jnp.stack(values, axis=0)] * n_row
        for bit in reversed(bits_of(n_row)):
            for k in range(0, n_row, 2 * bit):
                pieces[k ^ bit] = swap(pieces[k], "row", bit)
        out = []
        for j, value in enumerate(values):
            full = jnp.zeros((n_row, rows, width), value.dtype)
            full = lax.dynamic_update_slice(full, value[None], (index, 0, 0))
            for k in range(1, n_row):
                full = lax.dynamic_update_slice(full, pieces[k][j][None], (index ^ k, 0, 0))
            out.append(full.reshape(n_row * rows, width))
        return out

    def reduce_weights(grads):
        total_rows, width = grads[0].shape
        rows = total_rows // n_row
        halves = [grad.astype(BF).reshape(n_row, rows, width) for grad in grads]
        blocks = [jnp.stack([half[k] for half in halves], axis=0) for k in range(n_row)]
        share = tree_scatter(reorder(blocks, "row"), "row", BF)
        bits = bits_of(n_img)
        for bit in bits:
            share = share.astype(F32) + swap(share, "img", bit).astype(F32)
            if bit != bits[-1]:
                share = share.astype(BF)
        share = share.astype(F32)
        return [share[k] for k in range(len(grads))]

    def body(
        tokens,
        attn_bias,
        first_gain,
        first_shift,
        qkv_weight,
        qkv_bias,
        proj_weight,
        proj_bias,
        scale_attn,
        second_gain,
        second_shift,
        fc1_weight,
        fc1_bias,
        fc2_weight,
        fc2_bias,
        scale_mlp,
        cotangent,
    ):
        count_rows, width = tokens.shape
        images = range(count_rows // SEQ)
        model = width * n_col
        head_count = qkv_weight.shape[2] // HEAD_DIM
        score_scale = HEAD_DIM ** (-0.5)
        bias_f = attn_bias.astype(F32)

        cot = [cotangent[g * SEQ : (g + 1) * SEQ] for g in images]
        rows_of = lambda a, g: a[g * SEQ : (g + 1) * SEQ]

        x_full = gather_cols(tokens)
        vectors = jnp.stack(
            [first_gain, first_shift, second_gain, second_shift, proj_bias, scale_attn, scale_mlp],
            axis=0,
        )
        vec_full = gather_cols(vectors)
        gain_one, shift_one, gain_two, shift_two, bias_proj, scale_one, scale_two = (
            vec_full[k][None] for k in range(7)
        )
        w_q, w_k, w_v, w_proj = gather_rows(
            [qkv_weight[:, 0], qkv_weight[:, 1], qkv_weight[:, 2], proj_weight]
        )
        grad_mlp = gather_cols((cotangent * scale_mlp).astype(BF))
        w_fc1, w_fc2 = gather_rows([fc1_weight, fc2_weight])

        def norm_stats(full):
            mean = jnp.mean(full, axis=1, keepdims=True)
            var = jnp.mean(full * full, axis=1, keepdims=True) - mean * mean
            return mean, lax.rsqrt(var + EPS)

        full = x_full.astype(F32)
        mean_one, inv_one = norm_stats(full)
        hat_one = (full - mean_one) * inv_one
        hat_one_own = (tokens.astype(F32) - mean_one) * inv_one
        norm_one = (hat_one * gain_one + shift_one).astype(BF)
        q_all = (dot(norm_one, w_q, ((1,), (0,))) + qkv_bias[0]).astype(BF)
        k_all = dot(norm_one, w_k, ((1,), (0,))).astype(BF)
        v_all = (dot(norm_one, w_v, ((1,), (0,))) + qkv_bias[1]).astype(BF)
        heads = lambda a: a.reshape(SEQ, head_count, HEAD_DIM)

        attn_out, log_total, proj_sum = [], [], []
        q_in, k_in, v_in = ([heads(rows_of(a, g)) for g in images] for a in (q_all, k_all, v_all))
        x_mid, proj_val, hat_two, hat_two_own, inv_two, norm_two = [], [], [], [], [], []
        for g in images:
            scores = (
                jnp.einsum("qhe,khe->hqk", q_in[g], k_in[g], preferred_element_type=F32) * score_scale
                + bias_f
            )
            row_max = jnp.max(scores, axis=-1, keepdims=True)
            log_sum = row_max + jnp.log(jnp.sum(jnp.exp(scores - row_max), axis=-1, keepdims=True))
            log_total.append(log_sum)
            weights_half = jnp.exp(scores - log_sum).astype(BF)
            out = jnp.einsum("hqk,khe->qhe", weights_half, v_in[g], preferred_element_type=F32)
            attn_out.append(out.reshape(SEQ, head_count * HEAD_DIM).astype(BF))
            proj_sum.append(scatter_cols(dot(attn_out[g], w_proj, ((1,), (1,)))))
        for g in images:
            proj_val.append(proj_sum[g] + proj_bias)
            x_mid.append(rows_of(tokens, g).astype(F32) + scale_attn * proj_val[g])
            gathered = gather_cols(proj_sum[g].astype(BF)).astype(F32)
            full = rows_of(x_full, g).astype(F32) + scale_one * (gathered + bias_proj)
            mean, inv = norm_stats(full)
            hat = (full - mean) * inv
            hat_two.append(hat)
            inv_two.append(inv)
            hat_two_own.append((x_mid[g] - mean) * inv)
            norm_two.append((hat * gain_two + shift_two).astype(BF))

        grad_pre, act_val, grad_two, grad_mid, grad_attn_in = [], [], [], [], []
        for g in images:
            pre = dot(norm_two[g], w_fc1, ((1,), (0,))) + fc1_bias
            gate = 0.5 * (1.0 + lax.erf(pre * SQRT_HALF))
            act_val.append((pre * gate).astype(BF))
            slope = gate + pre * jnp.exp(-0.5 * pre * pre) * INV_ROOT_TWO_PI
            grad_act = dot(rows_of(grad_mlp, g), w_fc2, ((1,), (0,)))
            grad_pre.append((grad_act * slope).astype(BF))
            grad_two.append(scatter_cols(dot(grad_pre[g], w_fc1, ((1,), (1,)))))
        for g in images:
            full = gather_cols(grad_two[g].astype(BF)).astype(F32) * gain_two
            total_one = jnp.mean(full, axis=1, keepdims=True)
            total_two = jnp.mean(full * hat_two[g], axis=1, keepdims=True)
            grad_mid.append(
                cot[g]
                + inv_two[g] * (grad_two[g] * second_gain - total_one - hat_two_own[g] * total_two)
            )
            mid_full = rows_of(grad_mlp, g).astype(F32) / scale_two + inv_two[g] * (
                full - total_one - hat_two[g] * total_two
            )
            grad_attn_in.append((mid_full * scale_one).astype(BF))

        grad_q, grad_k, grad_v, grad_one, totals = [], [], [], [], []
        for g in images:
            grad_heads = dot(grad_attn_in[g], w_proj, ((1,), (0,))).astype(BF)
            d_out = heads(grad_heads)
            scores = (
                jnp.einsum("qhe,khe->hqk", q_in[g], k_in[g], preferred_element_type=F32) * score_scale
                + bias_f
            )
            prob = jnp.exp(scores - log_total[g])
            prob_half = prob.astype(BF)
            d_v = jnp.einsum("hqk,qhe->khe", prob_half, d_out, preferred_element_type=F32)
            d_p = jnp.einsum("qhe,khe->hqk", d_out, v_in[g], preferred_element_type=F32)
            row_dot = jnp.sum(prob * d_p, axis=-1, keepdims=True)
            d_s = (prob * (d_p - row_dot)).astype(BF)
            d_q = jnp.einsum("hqk,khe->qhe", d_s, k_in[g], preferred_element_type=F32)
            d_k = jnp.einsum("hqk,qhe->khe", d_s, q_in[g], preferred_element_type=F32)
            flat = lambda a: a.reshape(SEQ, head_count * HEAD_DIM).astype(BF)
            grad_q.append(flat(d_q * score_scale))
            grad_k.append(flat(d_k * score_scale))
            grad_v.append(flat(d_v))
            part = (
                dot(grad_q[g], w_q, ((1,), (1,)))
                + dot(grad_k[g], w_k, ((1,), (1,)))
                + dot(grad_v[g], w_v, ((1,), (1,)))
            )
            scaled = part * gain_one
            totals += [jnp.sum(scaled, axis=1), jnp.sum(scaled * rows_of(hat_one, g), axis=1)]
            grad_one.append(scatter_cols(part))
        totals = all_sum(jnp.stack(totals, axis=0), ("col",)) / model
        grad_tokens = [
            grad_mid[g]
            + rows_of(inv_one, g)
            * (
                grad_one[g] * first_gain
                - totals[2 * g][:, None]
                - rows_of(hat_one_own, g) * totals[2 * g + 1][:, None]
            )
            for g in images
        ]

        def over_tokens(left, right):
            return dot(left, jnp.concatenate(right, axis=0), ((0,), (0,)))

        whole = lambda a: jnp.concatenate(a, axis=0)
        grad_fc1, grad_fc2 = reduce_weights(
            [over_tokens(whole(norm_two), grad_pre), over_tokens(grad_mlp, act_val)]
        )
        *grad_qkv, grad_proj = reduce_weights(
            [over_tokens(norm_one, d) for d in (grad_q, grad_k, grad_v)]
            + [over_tokens(whole(grad_attn_in), attn_out)]
        )
        grad_qkv = jnp.stack(grad_qkv, axis=0)

        mlp_all = dot(whole(act_val), w_fc2, ((1,), (1,)))
        mlp_val = scatter_cols(mlp_all) + fc2_bias
        out_y = whole(x_mid) + scale_mlp * mlp_val

        def token_sum(terms):
            return sum(jnp.sum(t.astype(F32), axis=0) for t in terms)

        sums = [
            token_sum(grad_q),
            token_sum(grad_v),
            token_sum([grad_mid[g] * scale_attn for g in images]),
            token_sum([grad_mid[g] * proj_val[g] for g in images]),
            token_sum([cotangent * scale_mlp]),
            token_sum([cotangent * mlp_val]),
            token_sum([grad_one[g] * rows_of(hat_one_own, g) for g in images]),
            token_sum(grad_one),
            token_sum([grad_two[g] * hat_two_own[g] for g in images]),
            token_sum(grad_two),
        ]
        sums = jnp.stack(sums + list(token_sum(grad_pre).reshape(-1, width)), axis=0)
        sums = all_sum(sums, ("row", "img"))
        sum_pre = sums[10:].reshape(-1)
        return (
            out_y,
            jnp.concatenate(grad_tokens, axis=0),
            jnp.transpose(grad_qkv, (1, 0, 2)),
            sums[:2],
            grad_proj,
            sums[2],
            sums[3],
            grad_fc1,
            sum_pre,
            grad_fc2,
            sums[4],
            sums[5],
            sums[6],
            sums[7],
            sums[8],
            sums[9],
        )

    return body


def solution(mesh):
    return jax.shard_map(
        make_body(mesh.shape["img"], mesh.shape["row"], mesh.shape["col"]),
        mesh=mesh,
        in_specs=(
            P(("img", "row"), "col"),
            P("col", None, None),
            P("col"),
            P("col"),
            P("row", None, "col"),
            P(None, "col"),
            P("row", "col"),
            P("col"),
            P("col"),
            P("col"),
            P("col"),
            P("row", "col"),
            P("col"),
            P("row", "col"),
            P("col"),
            P("col"),
            P(("img", "row"), "col"),
        ),
        out_specs=(
            P(("img", "row"), "col"),
            P(("img", "row"), "col"),
            P("row", None, "col"),
            P(None, "col"),
            P("row", "col"),
            P("col"),
            P("col"),
            P("row", "col"),
            P("col"),
            P("row", "col"),
            P("col"),
            P("col"),
            P("col"),
            P("col"),
            P("col"),
            P("col"),
        ),
        check_vma=False,
    )
```

```python
import functools

import jax
import jax.numpy as jnp
from jax import lax
from jax.experimental import pallas as pl
from jax.experimental.pallas import tpu as pltpu
from jax.sharding import PartitionSpec as P

HEAD_DIM = 64
SEQ = 257
ROWS = (SEQ + 15) // 16 * 16
EPS = 1e-06
SQRT_HALF = 0.7071067811865476
INV_ROOT_TWO_PI = 0.3989422804014327
MASKED = -1e30

BF = jnp.bfloat16
F32 = jnp.float32


def dot(left, right, dims=((1,), (0,))):
    return lax.dot_general(left, right, (dims, ((), ())), preferred_element_type=F32)


def dot_last(left, right):
    return dot(left, right, ((1,), (1,)))


def dot_first(left, right):
    return dot(left, right, ((0,), (0,)))


def bits_of(count):
    out = []
    bit = 1
    while bit < count:
        out.append(bit)
        bit *= 2
    return out


def tree_order(count):
    order = [0]
    for bit in reversed(bits_of(count)):
        order = order + [m | bit for m in order]
    return order


class Blocks:
    def __init__(self, low, high):
        self.low, self.high = low, high
        self.half = low.shape[0]
        self.order = tree_order(2 * self.half)

    def at(self, mask):
        place = self.order.index(mask)
        return self.low[place] if place < self.half else self.high[place - self.half]

    def put(self, mask, value):
        place = self.order.index(mask)
        if place < self.half:
            self.low[place] = value
        else:
            self.high[place - self.half] = value


def span(col, mask, width):
    return pl.ds(pl.multiple_of((col ^ mask) * width, width), width)


GAIN_ONE, SHIFT_ONE, GAIN_TWO, SHIFT_TWO, BIAS_PROJ, SCALE_ONE, SCALE_TWO = range(7)


def vec_at(vecs, mask, which):
    return vecs.at(mask)[which : which + 1]


def norm_all(blocks, model):
    mean = sum(jnp.sum(b, axis=1, keepdims=True) for b in blocks) / model
    var = sum(jnp.sum(b * b, axis=1, keepdims=True) for b in blocks) / model - mean * mean
    inv = lax.rsqrt(var + EPS)
    return [(b - mean) * inv for b in blocks], inv


def probs_of(q, k, bias):
    scores = dot_last(q, k) * (HEAD_DIM ** (-0.5)) + bias
    top = jnp.max(scores, axis=-1, keepdims=True)
    raised = jnp.exp(scores - top)
    return raised * (1.0 / jnp.sum(raised, axis=-1, keepdims=True))


def front_kernel(
    n, at, x_lo, x_hi, v_lo, v_hi, w_qkv, qkv_bias, bias, w_proj, norm_o, qkv_o, attn_o, keep_o, send_o
):
    col = at[0]
    x, vecs, out = Blocks(x_lo, x_hi), Blocks(v_lo, v_hi), Blocks(keep_o, send_o)
    width = x_lo.shape[2]
    hats, _ = norm_all([x.at(m).astype(F32) for m in range(n)], n * width)
    sums = [None] * 3
    for m in range(n):
        rows = span(col, m, width)
        norm = (hats[m] * vec_at(vecs, m, GAIN_ONE) + vec_at(vecs, m, SHIFT_ONE)).astype(BF)
        norm_o[:, rows] = norm
        for j in range(3):
            term = dot(norm, w_qkv[j, rows, :])
            sums[j] = term if m == 0 else sums[j] + term
    qkv = [
        (sums[0] + qkv_bias[0:1]).astype(BF),
        sums[1].astype(BF),
        (sums[2] + qkv_bias[1:2]).astype(BF),
    ]
    for j in range(3):
        qkv_o[j] = qkv[j]
    outs = []
    for h in range(bias.shape[0]):
        part = slice(h * HEAD_DIM, (h + 1) * HEAD_DIM)
        weights = probs_of(qkv[0][:, part], qkv[1][:, part], bias[h].astype(F32))
        outs.append(dot(weights.astype(BF), qkv[2][:, part]))
    attn = jnp.concatenate(outs, axis=1).astype(BF)
    attn_o[...] = attn
    for m in range(n):
        out.put(m, dot_last(attn, w_proj[span(col, m, width), :]).astype(BF))


def middle_kernel(
    n, at, x_lo, x_hi, p_lo, p_hi, g_lo, g_hi, v_lo, v_hi, w_fc1, w_fc2, fc1_bias,
    hat_o, inv_o, norm_o, gmlp_o, act_o, pre_o, sum_o, keep_o, send_o,
):
    col = at[0]
    x, p, gm, vecs = Blocks(x_lo, x_hi), Blocks(p_lo, p_hi), Blocks(g_lo, g_hi), Blocks(v_lo, v_hi)
    out = Blocks(keep_o, send_o)
    width = x_lo.shape[2]
    mids = [
        x.at(m).astype(F32)
        + vec_at(vecs, m, SCALE_ONE) * (p.at(m).astype(F32) + vec_at(vecs, m, BIAS_PROJ))
        for m in range(n)
    ]
    hats, inv = norm_all(mids, n * width)
    inv_o[...] = jnp.broadcast_to(inv, inv_o.shape)
    pre, grad_act = None, None
    for m in range(n):
        rows = span(col, m, width)
        hat_o[m] = hats[m].astype(BF)
        norm = (hats[m] * vec_at(vecs, m, GAIN_TWO) + vec_at(vecs, m, SHIFT_TWO)).astype(BF)
        norm_o[:, rows] = norm
        grad_mlp = gm.at(m)
        gmlp_o[:, rows] = grad_mlp
        one, two = dot(norm, w_fc1[rows, :]), dot(grad_mlp, w_fc2[rows, :])
        pre, grad_act = (one, two) if m == 0 else (pre + one, grad_act + two)
    pre = pre + fc1_bias[...]
    gate = 0.5 * (1.0 + lax.erf(pre * SQRT_HALF))
    act_o[...] = (pre * gate).astype(BF)
    slope = gate + pre * jnp.exp(-0.5 * pre * pre) * INV_ROOT_TWO_PI
    grad_pre = (grad_act * slope).astype(BF)
    pre_o[...] = grad_pre
    sum_o[...] = jnp.sum(grad_pre.astype(F32), axis=0, keepdims=True)
    for m in range(n):
        out.put(m, dot_last(grad_pre, w_fc1[span(col, m, width), :]).astype(BF))


def mlp_kernel(n, at, act_a, act_b, w_fc2, keep_o, send_o):
    col = at[0]
    out = Blocks(keep_o, send_o)
    width = keep_o.shape[3]
    for m in range(n):
        rows = w_fc2[span(col, m, width), :]
        out.put(m, jnp.stack([dot_last(a[...], rows).astype(BF) for a in (act_a, act_b)], axis=0))


def back_kernel(
    n, at, d_lo, d_hi, hat_two, inv_two, g_lo, g_hi, p_own, v_lo, v_hi, qkv, bias, w_proj, w_qkv, x_lo, x_hi,
    attn_in_o, mid_o, dqkv_o, sum_o, part_o, total_o, keep_o, send_o,
):
    col = at[0]
    x, gm, vecs = Blocks(x_lo, x_hi), Blocks(g_lo, g_hi), Blocks(v_lo, v_hi)
    d_two, out = Blocks(d_lo, d_hi), Blocks(keep_o, send_o)
    width = x_lo.shape[2]
    model = n * width
    scale = HEAD_DIM ** (-0.5)
    inv = inv_two[:, 0:1]
    scaled = [d_two.at(m).astype(F32) * vec_at(vecs, m, GAIN_TWO) for m in range(n)]
    hats = [hat_two[m].astype(F32) for m in range(n)]
    mean_one = sum(jnp.sum(s, axis=1, keepdims=True) for s in scaled) / model
    mean_two = sum(jnp.sum(s * h, axis=1, keepdims=True) for s, h in zip(scaled, hats)) / model
    grad_heads = None
    for m in range(n):
        rows = span(col, m, width)
        mid = gm.at(m).astype(F32) / vec_at(vecs, m, SCALE_TWO) + inv * (
            scaled[m] - mean_one - hats[m] * mean_two
        )
        biased = mid * vec_at(vecs, m, SCALE_ONE)
        attn_in = biased.astype(BF)
        attn_in_o[:, rows] = attn_in
        term = dot(attn_in, w_proj[rows, :])
        grad_heads = term if m == 0 else grad_heads + term
        if m == 0:
            mid_o[...] = mid
            d_own = d_two.at(0).astype(F32)
            proj_val = p_own[0].astype(F32) + vec_at(vecs, 0, BIAS_PROJ)
            for place, value in ((2, biased), (3, mid * proj_val), (4, d_own * hats[0]), (5, d_own)):
                sum_o[place : place + 1, :] = jnp.sum(value, axis=0, keepdims=True)
    grad_heads = grad_heads.astype(BF)
    parts = [[], [], []]
    for h in range(bias.shape[0]):
        part = slice(h * HEAD_DIM, (h + 1) * HEAD_DIM)
        q, k, v = (qkv[j][:, part] for j in range(3))
        d_out = grad_heads[:, part]
        prob = probs_of(q, k, bias[h].astype(F32))
        grad_p = dot_last(d_out, v)
        row_dot = jnp.sum(prob * grad_p, axis=-1, keepdims=True)
        grad_s = (prob * (grad_p - row_dot)).astype(BF)
        parts[0].append(dot(grad_s, k) * scale)
        parts[1].append(dot_first(grad_s, q) * scale)
        parts[2].append(dot_first(prob.astype(BF), d_out))
    grads = [jnp.concatenate(p, axis=1).astype(BF) for p in parts]
    for j in range(3):
        dqkv_o[j] = grads[j]
    for place, j in ((0, 0), (1, 2)):
        sum_o[place : place + 1, :] = jnp.sum(grads[j].astype(F32), axis=0, keepdims=True)
    sum_o[6:8, :] = jnp.zeros((2, width), F32)
    hats, _ = norm_all([x.at(m).astype(F32) for m in range(n)], model)
    total_one, total_two = 0.0, 0.0
    for m in range(n):
        rows = span(col, m, width)
        full = sum(dot_last(grads[j], w_qkv[j, rows, :]) for j in range(3))
        out.put(m, full.astype(BF))
        hatted = full * hats[m]
        gain = vec_at(vecs, m, GAIN_ONE)
        total_one = total_one + jnp.sum(full * gain, axis=1, keepdims=True)
        total_two = total_two + jnp.sum(hatted * gain, axis=1, keepdims=True)
        place = tree_order(n).index(m)
        part_o[place, 0:1, :] = jnp.sum(hatted, axis=0, keepdims=True)
        part_o[place, 1:2, :] = jnp.sum(full, axis=0, keepdims=True)
    lane = lax.broadcasted_iota(jnp.int32, total_o.shape, 1)
    total_o[...] = jnp.where(lane == 0, total_one, total_two)


def weight_kernel(n, pairs, at, *refs):
    row = at[1]
    left_a, left_b, right_a, right_b = (refs[i * pairs : (i + 1) * pairs] for i in range(4))
    out = Blocks(refs[4 * pairs], refs[4 * pairs + 1])
    rows = refs[4 * pairs].shape[2]
    for m in range(n):
        where = span(row, m, rows)
        out.put(
            m,
            jnp.stack(
                [
                    (
                        dot_first(left_a[j][:, where], right_a[j][...])
                        + dot_first(left_b[j][:, where], right_b[j][...])
                    ).astype(BF)
                    for j in range(pairs)
                ],
                axis=0,
            ),
        )


def kernel_call(body, name, outs, at, *args, flops=0):
    vmem = pl.BlockSpec(memory_space=pltpu.VMEM)
    return pl.pallas_call(
        body,
        name=name,
        out_shape=[jax.ShapeDtypeStruct(shape, kind) for shape, kind in outs],
        in_specs=[pl.BlockSpec(memory_space=pltpu.SMEM)] + [vmem] * len(args),
        out_specs=[vmem] * len(outs),
        compiler_params=pltpu.CompilerParams(vmem_limit_bytes=40 * 2**20),
    )(at, *args)


def make_body(n_img, n_row, n_col):
    sizes = {"img": n_img, "row": n_row, "col": n_col}

    def swap(value, axis, mask):
        return lax.ppermute(value, axis, [(i, i ^ mask) for i in range(sizes[axis])])

    def gather_blocks(value):
        held = value[None]
        for bit in reversed(bits_of(n_col)):
            got = swap(held, "col", bit)
            if bit == 1:
                return held, got
            held = jnp.concatenate([held, got], axis=0)

    def scatter_blocks(keep, send, axis):
        bits = bits_of(sizes[axis])
        half = keep.shape[0]
        held = [keep]
        for bit in bits:
            held.append(swap(send, axis, bit))
            if bit != bits[-1]:
                half //= 2
                send = sum(h[half : 2 * half].astype(F32) for h in held).astype(keep.dtype)
        return sum(h[0].astype(F32) for h in held)

    def all_sum(value, axes):
        for axis in axes:
            for bit in bits_of(sizes[axis]):
                value = value + swap(value, axis, bit)
        return value

    def gather_rows(values):
        index = lax.axis_index("row")
        rows, width = values[0].shape
        pieces = [jnp.stack(values, axis=0)] * n_row
        for bit in reversed(bits_of(n_row)):
            for k in range(0, n_row, 2 * bit):
                pieces[k ^ bit] = swap(pieces[k], "row", bit)
        full = jnp.zeros((len(values), n_row, rows, width), values[0].dtype)
        for k in range(n_row):
            full = lax.dynamic_update_slice(full, pieces[k][:, None], (0, index ^ k, 0, 0))
        return full.reshape(len(values), n_row * rows, width)

    def sum_img(share):
        bits = bits_of(n_img)
        share = share.astype(BF)
        for bit in bits:
            share = share.astype(F32) + swap(share, "img", bit).astype(F32)
            if bit != bits[-1]:
                share = share.astype(BF)
        return share.astype(F32)

    def body(
        tokens,
        attn_bias,
        first_gain,
        first_shift,
        qkv_weight,
        qkv_bias,
        proj_weight,
        proj_bias,
        scale_attn,
        second_gain,
        second_shift,
        fc1_weight,
        fc1_bias,
        fc2_weight,
        fc2_bias,
        scale_mlp,
        cotangent,
    ):
        count_rows, width = tokens.shape
        images = range(count_rows // SEQ)
        model = width * n_col
        hidden = fc1_weight.shape[1]
        head_count = attn_bias.shape[0]
        half = n_col // 2
        at = jnp.stack([lax.axis_index("col"), lax.axis_index("row")]).astype(jnp.int32)

        def padded(value, g):
            return jnp.pad(value[g * SEQ : (g + 1) * SEQ], ((0, ROWS - SEQ), (0, 0)))

        x_own = [padded(tokens, g) for g in images]
        x_got = [gather_blocks(x_own[g]) for g in images]
        vectors = jnp.stack(
            [
                first_gain,
                first_shift,
                second_gain,
                second_shift,
                proj_bias,
                scale_attn,
                scale_mlp,
                scale_mlp,
            ],
            axis=0,
        )
        vecs = gather_blocks(vectors)
        weights = gather_rows([qkv_weight[:, 0], qkv_weight[:, 1], qkv_weight[:, 2], proj_weight])
        w_qkv, w_proj = weights[:3], weights[3]
        gm_own = (cotangent * scale_mlp).astype(BF)
        gm_got = [gather_blocks(padded(gm_own, g)) for g in images]
        w_fc1, w_fc2 = gather_rows([fc1_weight, fc2_weight])
        bias = jnp.pad(attn_bias, ((0, 0), (0, 0), (0, ROWS - SEQ)), constant_values=MASKED)
        bias = jnp.pad(bias, ((0, 0), (0, ROWS - SEQ), (0, 0)))

        stack = ((half, ROWS, width), BF)
        wide = ((ROWS, model), BF)
        front, p_sum, p_got = [], [], []
        for g in images:
            with jax.named_scope(f"front_{g}"):
                front.append(
                    kernel_call(
                        functools.partial(front_kernel, n_col),
                        f"front{g}",
                        [wide, ((3, ROWS, width), BF), ((ROWS, width), BF), stack, stack],
                        at, *x_got[g], *vecs, w_qkv, qkv_bias, bias, w_proj,
                    )
                )
            p_sum.append(scatter_blocks(front[g][3], front[g][4], "col"))
            p_got.append(gather_blocks(p_sum[g].astype(BF)))

        middle, d_sum, d_got = [], [], []
        for g in images:
            with jax.named_scope(f"middle_{g}"):
                middle.append(
                    kernel_call(
                        functools.partial(middle_kernel, n_col),
                        f"middle{g}",
                        [
                            ((n_col, ROWS, width), BF), ((ROWS, 128), F32), wide, wide,
                            ((ROWS, hidden), BF), ((ROWS, hidden), BF), ((1, hidden), F32), stack, stack,
                        ],
                        at, *x_got[g], *p_got[g], *gm_got[g], *vecs, w_fc1, w_fc2, fc1_bias[None],
                    )
                )
            d_sum.append(scatter_blocks(middle[g][7], middle[g][8], "col"))
            d_got.append(gather_blocks(d_sum[g].astype(BF)))

        def weight_grads(name, lefts, rights):
            rows, cols = lefts[0][0].shape[1] // n_row, rights[0][0].shape[1]
            shape = ((n_row // 2, len(lefts), rows, cols), BF)
            keep, send = kernel_call(
                functools.partial(weight_kernel, n_row, len(lefts)),
                name,
                [shape, shape],
                at,
                *[t[g] for g in images for t in lefts],
                *[t[g] for g in images for t in rights],
            )
            return sum_img(scatter_blocks(keep, send, "row"))

        each = lambda results, k: [results[g][k] for g in images]
        with jax.named_scope("weights_fc"):
            grad_fc = weight_grads(
                "weights_fc",
                [each(middle, 2), each(middle, 3)],
                [each(middle, 5), each(middle, 4)],
            )

        back = []
        for g in images:
            with jax.named_scope(f"back_{g}"):
                back.append(
                    kernel_call(
                        functools.partial(back_kernel, n_col),
                        f"back{g}",
                        [
                            wide, ((ROWS, width), F32), ((3, ROWS, width), BF), ((8, width), F32),
                            ((n_col, 2, width), F32), ((ROWS, 128), F32), stack, stack,
                        ],
                        at, *d_got[g], middle[g][0], middle[g][1], *gm_got[g], p_got[g][0], *vecs,
                        front[g][1], bias, w_proj, w_qkv, *x_got[g],
                    )
                )
        grad_one = [scatter_blocks(back[g][6], back[g][7], "col") for g in images]
        totals = jnp.concatenate([back[g][5][:, :2].T for g in images], axis=0)
        totals = all_sum(totals, ("col",)) / model

        shape = ((2 * half // 2, 2, ROWS, width), BF)
        with jax.named_scope("mlp"):
            mlp_keep, mlp_send = kernel_call(
                functools.partial(mlp_kernel, n_col),
                "mlp",
                [shape, shape],
                at, middle[0][4], middle[1][4], w_fc2,
            )
        mlp_sum = scatter_blocks(mlp_keep, mlp_send, "col")

        with jax.named_scope("weights_qkv"):
            grad_qkv = weight_grads(
                "weights_qkv",
                [each(front, 0)] * 3 + [each(back, 0)],
                [[back[g][2][j] for g in images] for j in range(3)] + [each(front, 2)],
            )

        join = lambda a: jnp.concatenate([v[:SEQ] for v in a], axis=0)
        mlp_val = join([mlp_sum[g] for g in images]) + fc2_bias
        x_val = tokens.astype(F32)
        out_y = x_val + scale_attn * (join(p_sum) + proj_bias) + scale_mlp * mlp_val

        grad_tokens = []
        for g in images:
            blocks = jnp.concatenate(x_got[g], axis=0).astype(F32)
            mean = jnp.sum(blocks, axis=(0, 2))[:, None] / model
            var = jnp.sum(blocks * blocks, axis=(0, 2))[:, None] / model - mean * mean
            inv = lax.rsqrt(var + EPS)
            hat = (x_own[g].astype(F32) - mean) * inv
            grad_tokens.append(
                back[g][1]
                + inv
                * (grad_one[g] * first_gain - totals[2 * g][:, None] - hat * totals[2 * g + 1][:, None])
            )

        early = jnp.stack([jnp.sum(cotangent * scale_mlp, axis=0), jnp.sum(cotangent * mlp_val, axis=0)])
        own = jnp.concatenate(
            [
                back[0][3][:6] + back[1][3][:6],
                early,
                (middle[0][6] + middle[1][6]).reshape(-1, width),
                (back[0][4] + back[1][4]).reshape(2 * n_col, width),
            ],
            axis=0,
        )
        own = all_sum(own, ("row", "img"))
        first = own[-2 * n_col :].reshape(2, half, 2, width)
        first = scatter_blocks(first[0], first[1], "col")
        sum_pre = own[8 : -2 * n_col].reshape(-1)
        return (
            out_y,
            join(grad_tokens),
            jnp.transpose(grad_qkv[:3], (1, 0, 2)),
            own[0:2],
            grad_qkv[3],
            own[2],
            own[3],
            grad_fc[0],
            sum_pre,
            grad_fc[1],
            own[6],
            own[7],
            first[0],
            first[1],
            own[4],
            own[5],
        )

    return body


def solution(mesh):
    return jax.shard_map(
        make_body(mesh.shape["img"], mesh.shape["row"], mesh.shape["col"]),
        mesh=mesh,
        in_specs=(
            P(("img", "row"), "col"),
            P("col", None, None),
            P("col"),
            P("col"),
            P("row", None, "col"),
            P(None, "col"),
            P("row", "col"),
            P("col"),
            P("col"),
            P("col"),
            P("col"),
            P("row", "col"),
            P("col"),
            P("row", "col"),
            P("col"),
            P("col"),
            P(("img", "row"), "col"),
        ),
        out_specs=(
            P(("img", "row"), "col"),
            P(("img", "row"), "col"),
            P("row", None, "col"),
            P(None, "col"),
            P("row", "col"),
            P("col"),
            P("col"),
            P("row", "col"),
            P("col"),
            P("row", "col"),
            P("col"),
            P("col"),
            P("col"),
            P("col"),
            P("col"),
            P("col"),
        ),
        check_vma=False,
    )
```

```python
import functools

import jax
import jax.numpy as jnp
from jax import lax
from jax.experimental import pallas as pl
from jax.experimental.pallas import tpu as pltpu
from jax.sharding import PartitionSpec as P


HEAD_DIM = 64
SEQ = 257
ROWS = (SEQ + 15) // 16 * 16
EPS = 1e-06
SQRT_HALF = 0.7071067811865476
INV_ROOT_TWO_PI = 0.3989422804014327
MASKED = -1e30

BF = jnp.bfloat16
F32 = jnp.float32


def dot(left, right, dims=((1,), (0,))):
    return lax.dot_general(left, right, (dims, ((), ())), preferred_element_type=F32)


def dot_last(left, right):
    return dot(left, right, ((1,), (1,)))


def dot_first(left, right):
    return dot(left, right, ((0,), (0,)))


def bits_of(count):
    out = []
    bit = 1
    while bit < count:
        out.append(bit)
        bit *= 2
    return out


def tree_order(count):
    order = [0]
    for bit in reversed(bits_of(count)):
        order = order + [m | bit for m in order]
    return order


class Blocks:
    def __init__(self, low, high):
        self.low, self.high = low, high
        self.half = low.shape[0]
        self.order = tree_order(2 * self.half)

    def at(self, mask):
        place = self.order.index(mask)
        return self.low[place] if place < self.half else self.high[place - self.half]

    def put(self, mask, value):
        place = self.order.index(mask)
        if place < self.half:
            self.low[place] = value
        else:
            self.high[place - self.half] = value


class Rows:
    def __init__(self, ref, at):
        self.ref, self.at = ref, at
        self.rows = ref.shape[2]

    def get(self, which, mask, width):
        start = (self.at[0] ^ mask) * width
        block = start // self.rows
        where = pl.ds(pl.multiple_of(start - block * self.rows, width), width)
        return self.ref[self.at[2 + block], which, where, :]


def span(col, mask, width):
    return pl.ds(pl.multiple_of((col ^ mask) * width, width), width)


GAIN_ONE, SHIFT_ONE, GAIN_TWO, SHIFT_TWO, BIAS_PROJ, SCALE_ONE, SCALE_TWO = range(7)


def vec_at(vecs, mask, which):
    return vecs.at(mask)[which : which + 1]


def norm_all(blocks, model):
    mean = sum(jnp.sum(b, axis=1, keepdims=True) for b in blocks) / model
    var = sum(jnp.sum(b * b, axis=1, keepdims=True) for b in blocks) / model - mean * mean
    inv = lax.rsqrt(var + EPS)
    return [(b - mean) * inv for b in blocks], inv


def probs_of(q, k, bias):
    scores = dot_last(q, k) * (HEAD_DIM ** (-0.5)) + bias
    top = jnp.max(scores, axis=-1, keepdims=True)
    raised = jnp.exp(scores - top)
    return raised * (1.0 / jnp.sum(raised, axis=-1, keepdims=True))


def front_kernel(
    n, at, x_lo, x_hi, v_lo, v_hi, w_attn, qkv_bias, bias, norm_o, qkv_o, attn_o, keep_o, send_o
):
    col = at[0]
    weights_of = Rows(w_attn, at)
    x, vecs, out = Blocks(x_lo, x_hi), Blocks(v_lo, v_hi), Blocks(keep_o, send_o)
    width = x_lo.shape[2]
    hats, _ = norm_all([x.at(m).astype(F32) for m in range(n)], n * width)
    sums = [None] * 3
    for m in range(n):
        rows = span(col, m, width)
        norm = (hats[m] * vec_at(vecs, m, GAIN_ONE) + vec_at(vecs, m, SHIFT_ONE)).astype(BF)
        norm_o[:, rows] = norm
        for j in range(3):
            term = dot(norm, weights_of.get(j, m, width))
            sums[j] = term if m == 0 else sums[j] + term
    qkv = [
        (sums[0] + qkv_bias[0:1]).astype(BF),
        sums[1].astype(BF),
        (sums[2] + qkv_bias[1:2]).astype(BF),
    ]
    for j in range(3):
        qkv_o[j] = qkv[j]
    outs = []
    for h in range(bias.shape[0]):
        part = slice(h * HEAD_DIM, (h + 1) * HEAD_DIM)
        weights = probs_of(qkv[0][:, part], qkv[1][:, part], bias[h].astype(F32))
        outs.append(dot(weights.astype(BF), qkv[2][:, part]))
    attn = jnp.concatenate(outs, axis=1).astype(BF)
    attn_o[...] = attn
    for m in range(n):
        out.put(m, dot_last(attn, weights_of.get(3, m, width)).astype(BF))


def middle_kernel(
    n, at, x_lo, x_hi, p_lo, p_hi, g_lo, g_hi, v_lo, v_hi, w_fc, fc1_bias,
    hat_o, inv_o, norm_o, gmlp_o, act_o, pre_o, sum_o, keep_o, send_o,
):
    col = at[0]
    weights_of = Rows(w_fc, at)
    x, p, gm, vecs = Blocks(x_lo, x_hi), Blocks(p_lo, p_hi), Blocks(g_lo, g_hi), Blocks(v_lo, v_hi)
    out = Blocks(keep_o, send_o)
    width = x_lo.shape[2]
    mids = [
        x.at(m).astype(F32)
        + vec_at(vecs, m, SCALE_ONE) * (p.at(m).astype(F32) + vec_at(vecs, m, BIAS_PROJ))
        for m in range(n)
    ]
    hats, inv = norm_all(mids, n * width)
    inv_o[...] = jnp.broadcast_to(inv, inv_o.shape)
    pre, grad_act = None, None
    for m in range(n):
        rows = span(col, m, width)
        hat_o[m] = hats[m].astype(BF)
        norm = (hats[m] * vec_at(vecs, m, GAIN_TWO) + vec_at(vecs, m, SHIFT_TWO)).astype(BF)
        norm_o[:, rows] = norm
        grad_mlp = gm.at(m)
        gmlp_o[:, rows] = grad_mlp
        one, two = dot(norm, weights_of.get(0, m, width)), dot(grad_mlp, weights_of.get(1, m, width))
        pre, grad_act = (one, two) if m == 0 else (pre + one, grad_act + two)
    pre = pre + fc1_bias[...]
    gate = 0.5 * (1.0 + lax.erf(pre * SQRT_HALF))
    act_o[...] = (pre * gate).astype(BF)
    slope = gate + pre * jnp.exp(-0.5 * pre * pre) * INV_ROOT_TWO_PI
    grad_pre = (grad_act * slope).astype(BF)
    pre_o[...] = grad_pre
    sum_o[...] = jnp.sum(grad_pre.astype(F32), axis=0, keepdims=True)
    for m in range(n):
        out.put(m, dot_last(grad_pre, weights_of.get(0, m, width)).astype(BF))


def mlp_kernel(n, at, act_a, act_b, ga_lo, ga_hi, gb_lo, gb_hi, v_lo, v_hi, w_fc, part_o, keep_o, send_o):
    weights_of = Rows(w_fc, at)
    vecs, out = Blocks(v_lo, v_hi), Blocks(keep_o, send_o)
    width = keep_o.shape[3]
    for m in range(n):
        rows = weights_of.get(1, m, width)
        total, halves = 0.0, []
        for act, gm in ((act_a, Blocks(ga_lo, ga_hi)), (act_b, Blocks(gb_lo, gb_hi))):
            product = dot_last(act[...], rows)
            halves.append(product.astype(BF))
            total = total + jnp.sum(product * gm.at(m).astype(F32), axis=0, keepdims=True)
        part_o[tree_order(n).index(m)] = total / vec_at(vecs, m, SCALE_TWO)
        out.put(m, jnp.stack(halves, axis=0))


def back_kernel(
    n, at, d_lo, d_hi, hat_two, inv_two, g_lo, g_hi, p_own, v_lo, v_hi, qkv, bias, w_attn, x_lo, x_hi,
    attn_in_o, mid_o, dqkv_o, sum_o, part_o, total_o, keep_o, send_o,
):
    col = at[0]
    x, gm, vecs = Blocks(x_lo, x_hi), Blocks(g_lo, g_hi), Blocks(v_lo, v_hi)
    d_two, out = Blocks(d_lo, d_hi), Blocks(keep_o, send_o)
    weights_of = Rows(w_attn, at)
    width = x_lo.shape[2]
    model = n * width
    scale = HEAD_DIM ** (-0.5)
    inv = inv_two[:, 0:1]
    scaled = [d_two.at(m).astype(F32) * vec_at(vecs, m, GAIN_TWO) for m in range(n)]
    hats = [hat_two[m].astype(F32) for m in range(n)]
    mean_one = sum(jnp.sum(s, axis=1, keepdims=True) for s in scaled) / model
    mean_two = sum(jnp.sum(s * h, axis=1, keepdims=True) for s, h in zip(scaled, hats)) / model
    grad_heads = None
    for m in range(n):
        rows = span(col, m, width)
        mid = gm.at(m).astype(F32) / vec_at(vecs, m, SCALE_TWO) + inv * (
            scaled[m] - mean_one - hats[m] * mean_two
        )
        biased = mid * vec_at(vecs, m, SCALE_ONE)
        attn_in = biased.astype(BF)
        attn_in_o[:, rows] = attn_in
        term = dot(attn_in, weights_of.get(3, m, width))
        grad_heads = term if m == 0 else grad_heads + term
        if m == 0:
            mid_o[...] = mid
            d_own = d_two.at(0).astype(F32)
            proj_val = p_own[0].astype(F32) + vec_at(vecs, 0, BIAS_PROJ)
            for place, value in ((2, biased), (3, mid * proj_val), (4, d_own * hats[0]), (5, d_own)):
                sum_o[place : place + 1, :] = jnp.sum(value, axis=0, keepdims=True)
    grad_heads = grad_heads.astype(BF)
    parts = [[], [], []]
    for h in range(bias.shape[0]):
        part = slice(h * HEAD_DIM, (h + 1) * HEAD_DIM)
        q, k, v = (qkv[j][:, part] for j in range(3))
        d_out = grad_heads[:, part]
        prob = probs_of(q, k, bias[h].astype(F32))
        grad_p = dot_last(d_out, v)
        row_dot = jnp.sum(prob * grad_p, axis=-1, keepdims=True)
        grad_s = (prob * (grad_p - row_dot)).astype(BF)
        parts[0].append(dot(grad_s, k) * scale)
        parts[1].append(dot_first(grad_s, q) * scale)
        parts[2].append(dot_first(prob.astype(BF), d_out))
    grads = [jnp.concatenate(p, axis=1).astype(BF) for p in parts]
    for j in range(3):
        dqkv_o[j] = grads[j]
    for place, j in ((0, 0), (1, 2)):
        sum_o[place : place + 1, :] = jnp.sum(grads[j].astype(F32), axis=0, keepdims=True)
    sum_o[6:8, :] = jnp.zeros((2, width), F32)
    hats, _ = norm_all([x.at(m).astype(F32) for m in range(n)], model)
    total_one, total_two = 0.0, 0.0
    for m in range(n):
        full = sum(dot_last(grads[j], weights_of.get(j, m, width)) for j in range(3))
        out.put(m, full.astype(BF))
        hatted = full * hats[m]
        gain = vec_at(vecs, m, GAIN_ONE)
        total_one = total_one + jnp.sum(full * gain, axis=1, keepdims=True)
        total_two = total_two + jnp.sum(hatted * gain, axis=1, keepdims=True)
        place = tree_order(n).index(m)
        part_o[place, 0:1, :] = jnp.sum(hatted, axis=0, keepdims=True)
        part_o[place, 1:2, :] = jnp.sum(full, axis=0, keepdims=True)
    lane = lax.broadcasted_iota(jnp.int32, total_o.shape, 1)
    total_o[...] = jnp.where(lane == 0, total_one, total_two)


def weight_kernel(n, pairs, at, *refs):
    row = at[1]
    left_a, left_b, right_a, right_b = (refs[i * pairs : (i + 1) * pairs] for i in range(4))
    out = Blocks(refs[4 * pairs], refs[4 * pairs + 1])
    rows = refs[4 * pairs].shape[2]
    for m in range(n):
        where = span(row, m, rows)
        out.put(
            m,
            jnp.stack(
                [
                    (
                        dot_first(left_a[j][:, where], right_a[j][...])
                        + dot_first(left_b[j][:, where], right_b[j][...])
                    ).astype(BF)
                    for j in range(pairs)
                ],
                axis=0,
            ),
        )


def kernel_call(body, outs, at, *args, flops=0):
    vmem = pl.BlockSpec(memory_space=pltpu.VMEM)
    return pl.pallas_call(
        body,
        out_shape=[jax.ShapeDtypeStruct(shape, kind) for shape, kind in outs],
        in_specs=[pl.BlockSpec(memory_space=pltpu.SMEM)] + [vmem] * len(args),
        out_specs=[vmem] * len(outs),
        compiler_params=pltpu.CompilerParams(vmem_limit_bytes=20 * 2**20),
    )(at, *args)


def make_body(n_img, n_row, n_col):
    sizes = {"img": n_img, "row": n_row, "col": n_col}

    def swap(value, axis, mask):
        return lax.ppermute(value, axis, [(i, i ^ mask) for i in range(sizes[axis])])

    def gather_blocks(value):
        held = value[None]
        for bit in reversed(bits_of(n_col)):
            got = swap(held, "col", bit)
            if bit == 1:
                return held, got
            held = jnp.concatenate([held, got], axis=0)

    def scatter_blocks(keep, send, axis):
        bits = bits_of(sizes[axis])
        half = keep.shape[0]
        held = [keep]
        for bit in bits:
            held.append(swap(send, axis, bit))
            if bit != bits[-1]:
                half //= 2
                send = sum(h[half : 2 * half].astype(F32) for h in held).astype(keep.dtype)
        return sum(h[0].astype(F32) for h in held)

    def all_sum(value, axes):
        for axis in axes:
            for bit in bits_of(sizes[axis]):
                value = value + swap(value, axis, bit)
        return value

    def gather_rows(values):
        held = jnp.stack(values, axis=0)[None]
        for bit in reversed(bits_of(n_row)):
            held = jnp.concatenate([held, swap(held, "row", bit)], axis=0)
        return held

    def reduce_weights(keep, send, chunks):
        bits = bits_of(n_row)
        held = [keep, swap(send, "row", bits[0])]
        count = keep.shape[1]
        cuts = [(i * count // chunks, (i + 1) * count // chunks) for i in range(chunks)]
        shares = []
        for low, high in cuts:
            mine = [h[:, low:high] for h in held]
            half = keep.shape[0]
            for bit in bits[1:]:
                half //= 2
                give = sum(h[half : 2 * half].astype(F32) for h in mine).astype(BF)
                mine.append(swap(give, "row", bit))
            share = sum(h[0].astype(F32) for h in mine).astype(BF)
            for bit in bits_of(n_img):
                share = share.astype(BF)
                share = share.astype(F32) + swap(share, "img", bit).astype(F32)
            shares.append(share)
        return shares

    def body(
        tokens,
        attn_bias,
        first_gain,
        first_shift,
        qkv_weight,
        qkv_bias,
        proj_weight,
        proj_bias,
        scale_attn,
        second_gain,
        second_shift,
        fc1_weight,
        fc1_bias,
        fc2_weight,
        fc2_bias,
        scale_mlp,
        cotangent,
    ):
        count_rows, width = tokens.shape
        images = range(count_rows // SEQ)
        model = width * n_col
        hidden = fc1_weight.shape[1]
        half = n_col // 2
        row = lax.axis_index("row")
        order = tree_order(n_row)
        places = jnp.array([order.index(k) for k in range(n_row)], jnp.int32)
        at = jnp.concatenate(
            [
                jnp.stack([lax.axis_index("col"), row]).astype(jnp.int32),
                jnp.take(places, jnp.arange(n_row) ^ row),
            ]
        )

        def padded(value, g):
            return jnp.pad(value[g * SEQ : (g + 1) * SEQ], ((0, ROWS - SEQ), (0, 0)))

        x_own = [padded(tokens, g) for g in images]
        x_got = [gather_blocks(x_own[g]) for g in images]
        vectors = jnp.stack(
            [
                first_gain,
                first_shift,
                second_gain,
                second_shift,
                proj_bias,
                scale_attn,
                scale_mlp,
                scale_mlp,
            ],
            axis=0,
        )
        vecs = gather_blocks(vectors)
        w_attn = gather_rows([qkv_weight[:, 0], qkv_weight[:, 1], qkv_weight[:, 2], proj_weight])
        gm_own = (cotangent * scale_mlp).astype(BF)
        gm_got = [gather_blocks(padded(gm_own, g)) for g in images]
        w_fc = gather_rows([fc1_weight, fc2_weight])
        bias = jnp.pad(attn_bias, ((0, 0), (0, 0), (0, ROWS - SEQ)), constant_values=MASKED)
        bias = jnp.pad(bias, ((0, 0), (0, ROWS - SEQ), (0, 0)))

        stack = ((half, ROWS, width), BF)
        wide = ((ROWS, model), BF)
        front, p_sum, p_got = [], [], []
        for g in images:
            front.append(
                kernel_call(
                    functools.partial(front_kernel, n_col),
                    [wide, ((3, ROWS, width), BF), ((ROWS, width), BF), stack, stack],
                    at, *x_got[g], *vecs, w_attn, qkv_bias, bias,
                )
            )
            p_sum.append(scatter_blocks(front[g][3], front[g][4], "col"))
            p_got.append(gather_blocks(p_sum[g].astype(BF)))

        middle, d_sum, d_got = [], [], []
        for g in images:
            middle.append(
                kernel_call(
                    functools.partial(middle_kernel, n_col),
                    [
                        ((n_col, ROWS, width), BF), ((ROWS, 128), F32), wide, wide,
                        ((ROWS, hidden), BF), ((ROWS, hidden), BF), ((1, hidden), F32), stack, stack,
                    ],
                    at, *x_got[g], *p_got[g], *gm_got[g], *vecs, w_fc, fc1_bias[None],
                )
            )
            d_sum.append(scatter_blocks(middle[g][7], middle[g][8], "col"))
            d_got.append(gather_blocks(d_sum[g].astype(BF)))

        def weight_grads(chunks, lefts, rights):
            rows, cols = lefts[0][0].shape[1] // n_row, rights[0][0].shape[1]
            shape = ((n_row // 2, len(lefts), rows, cols), BF)
            keep, send = kernel_call(
                functools.partial(weight_kernel, n_row, len(lefts)),
                [shape, shape],
                at,
                *[t[g] for g in images for t in lefts],
                *[t[g] for g in images for t in rights],
            )
            return reduce_weights(keep, send, chunks)

        each = lambda results, k: [results[g][k] for g in images]
        (grad_fc,) = weight_grads(
            1, [each(middle, 2), each(middle, 3)], [each(middle, 5), each(middle, 4)]
        )

        shape = ((half, 2, ROWS, width), BF)
        mlp_part, mlp_keep, mlp_send = kernel_call(
            functools.partial(mlp_kernel, n_col),
            [((n_col, 1, width), F32), shape, shape],
            at, middle[0][4], middle[1][4], *gm_got[0], *gm_got[1], *vecs, w_fc,
        )

        back = []
        for g in images:
            back.append(
                kernel_call(
                    functools.partial(back_kernel, n_col),
                    [
                        wide, ((ROWS, width), F32), ((3, ROWS, width), BF), ((8, width), F32),
                        ((n_col, 2, width), F32), ((ROWS, 128), F32), stack, stack,
                    ],
                    at, *d_got[g], middle[g][0], middle[g][1], *gm_got[g], p_got[g][0], *vecs,
                    front[g][1], bias, w_attn, *x_got[g],
                )
            )
        grad_one = [scatter_blocks(back[g][6], back[g][7], "col") for g in images]
        totals = jnp.concatenate([back[g][5][:, :2].T for g in images], axis=0)
        totals = all_sum(totals, ("col",)) / model

        grad_attn = weight_grads(
            2,
            [each(front, 0)] * 3 + [each(back, 0)],
            [[back[g][2][j] for g in images] for j in range(3)] + [each(front, 2)],
        )
        grad_qkv = jnp.concatenate(grad_attn, axis=0)

        mlp_sum = scatter_blocks(mlp_keep, mlp_send, "col")

        join = lambda a: jnp.concatenate([v[:SEQ] for v in a], axis=0)
        mlp_val = join([mlp_sum[g] for g in images]) + fc2_bias
        x_val = tokens.astype(F32)
        out_y = x_val + scale_attn * (join(p_sum) + proj_bias) + scale_mlp * mlp_val

        grad_tokens = []
        for g in images:
            blocks = jnp.concatenate(x_got[g], axis=0).astype(F32)
            mean = jnp.sum(blocks, axis=(0, 2))[:, None] / model
            var = jnp.sum(blocks * blocks, axis=(0, 2))[:, None] / model - mean * mean
            inv = lax.rsqrt(var + EPS)
            hat = (x_own[g].astype(F32) - mean) * inv
            grad_tokens.append(
                back[g][1]
                + inv
                * (grad_one[g] * first_gain - totals[2 * g][:, None] - hat * totals[2 * g + 1][:, None])
            )

        cot_sum = jnp.sum(cotangent, axis=0)
        early = jnp.stack([cot_sum * scale_mlp, cot_sum * fc2_bias])
        parts = jnp.concatenate([back[0][4] + back[1][4], mlp_part], axis=1)
        own = jnp.concatenate(
            [
                back[0][3][:6] + back[1][3][:6],
                early,
                (middle[0][6] + middle[1][6]).reshape(-1, width),
                parts.reshape(3 * n_col, width),
            ],
            axis=0,
        )
        own = all_sum(own, ("row", "img"))
        first = own[-3 * n_col :].reshape(2, half, 3, width)
        first = scatter_blocks(first[0], first[1], "col")
        sum_pre = own[8 : -3 * n_col].reshape(-1)
        return (
            out_y,
            join(grad_tokens),
            jnp.transpose(grad_qkv[:3], (1, 0, 2)),
            own[0:2],
            grad_qkv[3],
            own[2],
            own[3],
            grad_fc[0],
            sum_pre,
            grad_fc[1],
            own[6],
            own[7] + first[2],
            first[0],
            first[1],
            own[4],
            own[5],
        )

    return body


def solution(mesh):
    counts = (mesh.shape["img"], mesh.shape["row"], mesh.shape["col"])
    step = sharded(mesh, make_body(*counts))
    return step


def sharded(mesh, body):
    return jax.shard_map(
        body,
        mesh=mesh,
        in_specs=(
            P(("img", "row"), "col"),
            P("col", None, None),
            P("col"),
            P("col"),
            P("row", None, "col"),
            P(None, "col"),
            P("row", "col"),
            P("col"),
            P("col"),
            P("col"),
            P("col"),
            P("row", "col"),
            P("col"),
            P("row", "col"),
            P("col"),
            P("col"),
            P(("img", "row"), "col"),
        ),
        out_specs=(
            P(("img", "row"), "col"),
            P(("img", "row"), "col"),
            P("row", None, "col"),
            P(None, "col"),
            P("row", "col"),
            P("col"),
            P("col"),
            P("row", "col"),
            P("col"),
            P("row", "col"),
            P("col"),
            P("col"),
            P("col"),
            P("col"),
            P("col"),
            P("col"),
        ),
        check_vma=False,
    )
```

```python
import functools

import jax
import jax.numpy as jnp
from jax import lax
from jax.experimental import pallas as pl
from jax.experimental.pallas import tpu as pltpu
from jax.sharding import PartitionSpec as P


HEAD_DIM = 64
SEQ = 257
ROWS = (SEQ + 15) // 16 * 16
EPS = 1e-06
SQRT_HALF = 0.7071067811865476
INV_ROOT_TWO_PI = 0.3989422804014327
MASKED = -1e30

BF = jnp.bfloat16
F32 = jnp.float32


def dot(left, right, dims=((1,), (0,))):
    return lax.dot_general(left, right, (dims, ((), ())), preferred_element_type=F32)


def dot_last(left, right):
    return dot(left, right, ((1,), (1,)))


def dot_first(left, right):
    return dot(left, right, ((0,), (0,)))


def bits_of(count):
    out = []
    bit = 1
    while bit < count:
        out.append(bit)
        bit *= 2
    return out


class Blocks:
    def __init__(self, refs):
        self.refs = refs

    def at(self, mask):
        return self.refs[mask][...]

    def put(self, mask, value):
        self.refs[mask][...] = value


def taker(refs):
    rest = list(refs)

    def take(count=None):
        got = [rest.pop(0) for _ in range(1 if count is None else count)]
        return got[0] if count is None else Blocks(got)

    return take


class Rows:
    def __init__(self, ref, at):
        self.ref, self.at = ref, at
        self.rows = ref.shape[2]

    def get(self, which, mask, width):
        start = (self.at[0] ^ mask) * width
        block = start // self.rows
        where = pl.ds(pl.multiple_of(start - block * self.rows, width), width)
        return self.ref[self.at[1] ^ block, which, where, :]


def span(col, mask, width):
    return pl.ds(pl.multiple_of((col ^ mask) * width, width), width)


GAIN_ONE, SHIFT_ONE, GAIN_TWO, SHIFT_TWO, BIAS_PROJ, SCALE_ONE, SCALE_TWO = range(7)


def vec_at(vecs, mask, which):
    return vecs.refs[mask][which : which + 1, :]


def norm_all(blocks, model):
    mean = sum(jnp.sum(b, axis=1, keepdims=True) for b in blocks) / model
    var = sum(jnp.sum(b * b, axis=1, keepdims=True) for b in blocks) / model - mean * mean
    inv = lax.rsqrt(var + EPS)
    return [(b - mean) * inv for b in blocks], inv


def probs_of(q, k, bias):
    scores = dot_last(q, k) * (HEAD_DIM ** (-0.5)) + bias
    top = jnp.max(scores, axis=-1, keepdims=True)
    raised = jnp.exp(scores - top)
    return raised * (1.0 / jnp.sum(raised, axis=-1, keepdims=True))


def front_kernel(n, at, *refs):
    col, take = at[0], taker(refs)
    x, vecs = take(n), take(n)
    w_attn, qkv_bias, bias, norm_o, qkv_o, attn_o = (take() for _ in range(6))
    out = take(n)
    weights_of = Rows(w_attn, at)
    width = x.refs[0].shape[1]
    hats, _ = norm_all([x.at(m).astype(F32) for m in range(n)], n * width)
    sums = [None] * 3
    for m in range(n):
        rows = span(col, m, width)
        norm = (hats[m] * vec_at(vecs, m, GAIN_ONE) + vec_at(vecs, m, SHIFT_ONE)).astype(BF)
        norm_o[:, rows] = norm
        for j in range(3):
            term = dot(norm, weights_of.get(j, m, width))
            sums[j] = term if m == 0 else sums[j] + term
    qkv = [
        (sums[0] + qkv_bias[0:1]).astype(BF),
        sums[1].astype(BF),
        (sums[2] + qkv_bias[1:2]).astype(BF),
    ]
    for j in range(3):
        qkv_o[j] = qkv[j]
    outs = []
    for h in range(bias.shape[0]):
        part = slice(h * HEAD_DIM, (h + 1) * HEAD_DIM)
        weights = probs_of(qkv[0][:, part], qkv[1][:, part], bias[h].astype(F32))
        outs.append(dot(weights.astype(BF), qkv[2][:, part]))
    attn = jnp.concatenate(outs, axis=1).astype(BF)
    attn_o[...] = attn
    for m in range(n):
        out.put(m, dot_last(attn, weights_of.get(3, m, width)).astype(BF))


def middle_kernel(n, g, at, *refs):
    col, take = at[0], taker(refs)
    x, p, gm, vecs = (take(n) for _ in range(4))
    w_fc, fc1_bias, hat_o, inv_o, norm_o, gmlp_o, act_o, pre_o, sum_o = (take() for _ in range(9))
    out = take(n)
    weights_of = Rows(w_fc, at)
    width = x.refs[0].shape[1]
    mids = [
        x.at(m).astype(F32)
        + vec_at(vecs, m, SCALE_ONE) * (p.at(m).astype(F32) + vec_at(vecs, m, BIAS_PROJ))
        for m in range(n)
    ]
    hats, inv = norm_all(mids, n * width)
    inv_o[...] = jnp.broadcast_to(inv, inv_o.shape)
    pre, grad_act = None, None
    for m in range(n):
        rows = span(col, m, width)
        hat_o[m] = hats[m].astype(BF)
        norm = (hats[m] * vec_at(vecs, m, GAIN_TWO) + vec_at(vecs, m, SHIFT_TWO)).astype(BF)
        norm_o[:, rows] = norm
        grad_mlp = gm.refs[m][g]
        gmlp_o[:, rows] = grad_mlp
        one, two = dot(norm, weights_of.get(0, m, width)), dot(grad_mlp, weights_of.get(1, m, width))
        pre, grad_act = (one, two) if m == 0 else (pre + one, grad_act + two)
    pre = pre + fc1_bias[...]
    gate = 0.5 * (1.0 + lax.erf(pre * SQRT_HALF))
    act_o[...] = (pre * gate).astype(BF)
    slope = gate + pre * jnp.exp(-0.5 * pre * pre) * INV_ROOT_TWO_PI
    grad_pre = (grad_act * slope).astype(BF)
    pre_o[...] = grad_pre
    sum_o[...] = jnp.sum(grad_pre.astype(F32), axis=0, keepdims=True)
    for m in range(n):
        out.put(m, dot_last(grad_pre, weights_of.get(0, m, width)).astype(BF))


def mlp_kernel(n, at, *refs):
    take = taker(refs)
    act_a, act_b, w_fc = take(), take(), take()
    out = take(n)
    weights_of = Rows(w_fc, at)
    width = out.refs[0].shape[2]
    for m in range(n):
        rows = weights_of.get(1, m, width)
        for j, act in enumerate((act_a, act_b)):
            out.refs[m][j] = dot_last(act[...], rows).astype(BF)


def back_kernel(n, g, at, *refs):
    col, take = at[0], taker(refs)
    d_two = take(n)
    hat_two, inv_two = take(), take()
    gm, p_own, vecs = take(n), take(), take(n)
    qkv, bias, w_attn = (take() for _ in range(3))
    x = take(n)
    before = [take() for _ in range(min(g, 1))]
    attn_in_o, mid_o, dqkv_o, sum_o, total_o = (take() for _ in range(5))
    out = take(n)
    weights_of = Rows(w_attn, at)
    width = x.refs[0].shape[1]
    model = n * width
    scale = HEAD_DIM ** (-0.5)
    inv = inv_two[:, 0:1]
    scaled = [d_two.at(m).astype(F32) * vec_at(vecs, m, GAIN_TWO) for m in range(n)]
    hats = [hat_two[m].astype(F32) for m in range(n)]
    mean_one = sum(jnp.sum(s, axis=1, keepdims=True) for s in scaled) / model
    mean_two = sum(jnp.sum(s * h, axis=1, keepdims=True) for s, h in zip(scaled, hats)) / model
    grad_heads = None
    for m in range(n):
        rows = span(col, m, width)
        mid = gm.refs[m][g].astype(F32) / vec_at(vecs, m, SCALE_TWO) + inv * (
            scaled[m] - mean_one - hats[m] * mean_two
        )
        biased = mid * vec_at(vecs, m, SCALE_ONE)
        attn_in = biased.astype(BF)
        attn_in_o[:, rows] = attn_in
        term = dot(attn_in, weights_of.get(3, m, width))
        grad_heads = term if m == 0 else grad_heads + term
        if m == 0:
            mid_o[...] = mid
            d_own = d_two.at(0).astype(F32)
            proj_val = p_own[...].astype(F32) + vec_at(vecs, 0, BIAS_PROJ)
            for place, value in ((2, biased), (3, mid * proj_val), (4, d_own * hats[0]), (5, d_own)):
                sum_o[place : place + 1, :] = jnp.sum(value, axis=0, keepdims=True)
    grad_heads = grad_heads.astype(BF)
    parts = [[], [], []]
    for h in range(bias.shape[0]):
        part = slice(h * HEAD_DIM, (h + 1) * HEAD_DIM)
        q, k, v = (qkv[j][:, part] for j in range(3))
        d_out = grad_heads[:, part]
        prob = probs_of(q, k, bias[h].astype(F32))
        grad_p = dot_last(d_out, v)
        row_dot = jnp.sum(prob * grad_p, axis=-1, keepdims=True)
        grad_s = (prob * (grad_p - row_dot)).astype(BF)
        parts[0].append(dot(grad_s, k) * scale)
        parts[1].append(dot_first(grad_s, q) * scale)
        parts[2].append(dot_first(prob.astype(BF), d_out))
    grads = [jnp.concatenate(p, axis=1).astype(BF) for p in parts]
    for j in range(3):
        dqkv_o[j] = grads[j]
    for place, j in ((0, 0), (1, 2)):
        sum_o[place : place + 1, :] = jnp.sum(grads[j].astype(F32), axis=0, keepdims=True)
    sum_o[6:8, :] = jnp.zeros((2, width), F32)
    hats, _ = norm_all([x.at(m).astype(F32) for m in range(n)], model)
    total_one, total_two = 0.0, 0.0
    for m in range(n):
        full = sum(dot_last(grads[j], weights_of.get(j, m, width)) for j in range(3))
        out.put(m, full.astype(BF))
        hatted = full * hats[m]
        gain = vec_at(vecs, m, GAIN_ONE)
        total_one = total_one + jnp.sum(full * gain, axis=1, keepdims=True)
        total_two = total_two + jnp.sum(hatted * gain, axis=1, keepdims=True)
    shape = (total_one.shape[0], 128)
    pair = jnp.where(lax.broadcasted_iota(jnp.int32, shape, 1) == 0, total_one, total_two)
    pick = lax.broadcasted_iota(jnp.int32, (8, 128), 0) == lax.broadcasted_iota(jnp.int32, (8, 128), 1)
    for ref in before:
        total_o[0 : 8 * g, :] = ref[...]
    total_o[8 * g : 8 * g + 8, :] = lax.dot_general(
        pick.astype(F32),
        pair,
        (((1,), (1,)), ((), ())),
        precision=lax.Precision.HIGHEST,
        preferred_element_type=F32,
    )


def weight_kernel(n, pairs, members, at, *refs):
    row = at[1]
    left_a, left_b, right_a, right_b = (refs[i * pairs : (i + 1) * pairs] for i in range(4))
    out = Blocks(refs[4 * pairs :])
    rows = out.refs[0].shape[1]
    for m in range(n):
        where = span(row, m, rows)
        for j, member in enumerate(members):
            pick = lambda ref: ref[...] if member is None else ref[member]
            out.refs[m][j] = (
                dot_first(left_a[j][:, where], pick(right_a[j]))
                + dot_first(left_b[j][:, where], pick(right_b[j]))
            ).astype(BF)


class Near:
    def __init__(self, value):
        self.value = value


def kernel_call(body, outs, at, *args):
    def placed(a):
        return a.value if isinstance(a, Near) else pltpu.with_memory_space_constraint(a, pltpu.HBM)

    return pl.pallas_call(
        body,
        out_shape=[pltpu.HBM(*o) for o in outs],
        in_specs=[pl.BlockSpec(memory_space=pltpu.SMEM)] + [pl.BlockSpec()] * len(args),
        out_specs=[pl.BlockSpec()] * len(outs),
        compiler_params=pltpu.CompilerParams(vmem_limit_bytes=40 * 2**20),
    )(at, *[placed(a) for a in args])


def make_body(n_img, n_row, n_col):
    sizes = {"img": n_img, "row": n_row, "col": n_col}

    def swap(value, axis, mask):
        return lax.ppermute(value, axis, [(i, i ^ mask) for i in range(sizes[axis])])

    def gather_blocks(value, axis="col"):
        pieces = [value] * sizes[axis]
        for m in range(1, sizes[axis]):
            low = m & -m
            pieces[m] = swap(pieces[m ^ low], axis, low)
        return pieces

    def scatter_blocks(blocks, axis):
        held = [[block] for block in blocks]
        for m in scatter_order(sizes[axis]):
            low = m & -m
            send = held[m][0]
            if len(held[m]) > 1:
                send = sum(h.astype(F32) for h in held[m]).astype(send.dtype)
            held[m ^ low].append(swap(send, axis, low))
        return sum(h.astype(F32) for h in held[0])

    def all_sum(value, axes):
        for axis in axes:
            for bit in bits_of(sizes[axis]):
                value = value + swap(value, axis, bit)
        return value

    def gather_rows(values):
        return jnp.stack(gather_blocks(jnp.stack(values, axis=0), "row"), axis=0)

    def reduce_weights(blocks):
        share = scatter_blocks(blocks, "row").astype(BF)
        img_bits = bits_of(n_img)
        for bit in img_bits[:-1]:
            share = share.astype(F32) + swap(share, "img", bit).astype(F32)
            share = share.astype(BF)
        got = swap(share, "img", img_bits[-1])
        return [share[k].astype(F32) + got[k].astype(F32) for k in range(share.shape[0])]

    def body(
        tokens,
        attn_bias,
        first_gain,
        first_shift,
        qkv_weight,
        qkv_bias,
        proj_weight,
        proj_bias,
        scale_attn,
        second_gain,
        second_shift,
        fc1_weight,
        fc1_bias,
        fc2_weight,
        fc2_bias,
        scale_mlp,
        cotangent,
    ):
        count_rows, width = tokens.shape
        images = range(count_rows // SEQ)
        model = width * n_col
        hidden = fc1_weight.shape[1]
        at = jnp.stack([lax.axis_index("col"), lax.axis_index("row")]).astype(jnp.int32)

        def padded(value, g):
            return jnp.pad(value[g * SEQ : (g + 1) * SEQ], ((0, ROWS - SEQ), (0, 0)))

        x_own = [padded(tokens, g) for g in images]
        x_got = [gather_blocks(x_own[g]) for g in images]
        vectors = jnp.stack(
            [
                first_gain,
                first_shift,
                second_gain,
                second_shift,
                proj_bias,
                scale_attn,
                scale_mlp,
                scale_mlp,
            ],
            axis=0,
        )
        vecs = gather_blocks(vectors)
        w_attn = gather_rows([qkv_weight[:, 0], qkv_weight[:, 1], qkv_weight[:, 2], proj_weight])
        late_cot, _ = lax.optimization_barrier((cotangent, x_got[0][1]))
        gm_own = (late_cot * scale_mlp).astype(BF)
        gm_got = gather_blocks(jnp.stack([padded(gm_own, g) for g in images]))
        w_fc = gather_rows([fc1_weight, fc2_weight])
        bias = jnp.pad(attn_bias, ((0, 0), (0, 0), (0, ROWS - SEQ)), constant_values=MASKED)
        bias = jnp.pad(bias, ((0, 0), (0, ROWS - SEQ), (0, 0)))

        blocks = [((ROWS, width), BF)] * n_col
        wide = ((ROWS, model), BF)
        front, p_sum, p_got = [], [], []
        for g in images:
            front.append(
                kernel_call(
                    functools.partial(front_kernel, n_col),
                    [wide, ((3, ROWS, width), BF), ((ROWS, width), BF), *blocks],
                    at, *x_got[g], *vecs, Near(w_attn), qkv_bias, Near(bias),
                )
            )
            p_sum.append(scatter_blocks(front[g][3:], "col"))
            p_got.append(gather_blocks(p_sum[g].astype(BF)))

        middle, d_sum, d_got = [], [], []
        for g in images:
            middle.append(
                kernel_call(
                    functools.partial(middle_kernel, n_col, g),
                    [
                        ((n_col, ROWS, width), BF), ((ROWS, 128), F32), wide, wide,
                        ((ROWS, hidden), BF), ((ROWS, hidden), BF), ((1, hidden), F32), *blocks,
                    ],
                    at, *x_got[g], *p_got[g], *gm_got, *vecs, Near(w_fc), fc1_bias[None],
                )
            )
            d_sum.append(scatter_blocks(middle[g][7:], "col"))
            d_got.append(gather_blocks(d_sum[g].astype(BF)))

        def weight_grads(lefts, rights, members):
            rows, cols = lefts[0][0].shape[1] // n_row, rights[0][0].shape[-1]
            parts = kernel_call(
                functools.partial(weight_kernel, n_row, len(lefts), members),
                [((len(lefts), rows, cols), BF)] * n_row,
                at,
                *[t[g] for g in images for t in lefts],
                *[t[g] for g in images for t in rights],
            )
            return reduce_weights(parts)

        each = lambda results, k: [results[g][k] for g in images]
        grad_fc1 = weight_grads([each(middle, 2)], [each(middle, 5)], [None])
        grad_fc2 = weight_grads([each(middle, 3)], [each(middle, 4)], [None])
        mlp_blocks = kernel_call(
            functools.partial(mlp_kernel, n_col),
            [((2, ROWS, width), BF)] * n_col,
            at, middle[0][4], middle[1][4], Near(w_fc),
        )

        back = []
        for g in images:
            back.append(
                kernel_call(
                    functools.partial(back_kernel, n_col, g),
                    [
                        wide, ((ROWS, width), F32), ((3, ROWS, width), BF), ((8, width), F32),
                        ((8 * g + 8, ROWS), F32), *blocks,
                    ],
                    at, *d_got[g], middle[g][0], middle[g][1], *gm_got, p_got[g][0], *vecs,
                    front[g][1], Near(bias), Near(w_attn), *x_got[g], *[b[4] for b in back[g - 1 : g]],
                )
            )
        grad_one = [scatter_blocks(back[g][5:], "col") for g in images]
        totals = back[-1][4]
        totals = all_sum(totals, ("col",)) / model

        d_qkv = each(back, 2)
        grad_qk = weight_grads([each(front, 0)] * 2, [d_qkv, d_qkv], [0, 1])
        grad_vp = weight_grads([each(front, 0), each(back, 0)], [d_qkv, each(front, 2)], [2, None])
        grad_qkv = jnp.stack([*grad_qk, grad_vp[0]], axis=0)
        mlp_sum = scatter_blocks(mlp_blocks, "col")

        join = lambda a: jnp.concatenate([v[:SEQ] for v in a], axis=0)
        mlp_val = join([mlp_sum[g] for g in images]) + fc2_bias
        x_val = tokens.astype(F32)
        out_y = x_val + scale_attn * (join(p_sum) + proj_bias) + scale_mlp * mlp_val

        grad_tokens, one_sums = [], []
        for g in images:
            hats, inv = norm_all([b.astype(F32) for b in x_got[g]], model)
            hat = hats[0]
            one_sums.append(jnp.stack([jnp.sum(grad_one[g] * hat, axis=0), jnp.sum(grad_one[g], axis=0)]))
            grad_tokens.append(
                back[g][1]
                + inv
                * (grad_one[g] * first_gain - totals[8 * g][:, None] - hat * totals[8 * g + 1][:, None])
            )

        last_cot, _ = lax.optimization_barrier((cotangent, back[0][3]))
        cot_sums = [jnp.sum(last_cot, axis=0) * scale_mlp, jnp.sum(last_cot * mlp_val, axis=0)]
        own = jnp.concatenate(
            [
                back[0][3][:6] + back[1][3][:6],
                jnp.stack(cot_sums),
                one_sums[0] + one_sums[1],
                (middle[0][6] + middle[1][6]).reshape(-1, width),
            ],
            axis=0,
        )
        own = all_sum(own, ("row", "img"))
        sum_pre = own[10:].reshape(-1)
        return (
            out_y,
            join(grad_tokens),
            jnp.transpose(grad_qkv, (1, 0, 2)),
            own[0:2],
            grad_vp[1],
            own[2],
            own[3],
            grad_fc1[0],
            sum_pre,
            grad_fc2[0],
            own[6],
            own[7],
            own[8],
            own[9],
            own[4],
            own[5],
        )

    return body


def scatter_order(count):
    return sorted(range(1, count), key=lambda m: (m & -m, -m))


def solution(mesh):
    counts = (mesh.shape["img"], mesh.shape["row"], mesh.shape["col"])
    step = sharded(mesh, make_body(*counts))
    return step


def sharded(mesh, body):
    return jax.shard_map(
        body,
        mesh=mesh,
        in_specs=(
            P(("img", "row"), "col"),
            P("col", None, None),
            P("col"),
            P("col"),
            P("row", None, "col"),
            P(None, "col"),
            P("row", "col"),
            P("col"),
            P("col"),
            P("col"),
            P("col"),
            P("row", "col"),
            P("col"),
            P("row", "col"),
            P("col"),
            P("col"),
            P(("img", "row"), "col"),
        ),
        out_specs=(
            P(("img", "row"), "col"),
            P(("img", "row"), "col"),
            P("row", None, "col"),
            P(None, "col"),
            P("row", "col"),
            P("col"),
            P("col"),
            P("row", "col"),
            P("col"),
            P("row", "col"),
            P("col"),
            P("col"),
            P("col"),
            P("col"),
            P("col"),
            P("col"),
        ),
        check_vma=False,
    )
```

```python
import functools

import jax
import jax.numpy as jnp
from jax import lax
from jax.experimental import pallas as pl
from jax.experimental.pallas import tpu as pltpu
from jax.sharding import PartitionSpec as P


HEAD_DIM = 64
SEQ = 257
ROWS = (SEQ + 15) // 16 * 16
EPS = 1e-06
SQRT_HALF = 0.7071067811865476
INV_ROOT_TWO_PI = 0.3989422804014327
MASKED = -1e30

BF = jnp.bfloat16
F32 = jnp.float32


def dot(left, right, dims=((1,), (0,))):
    return lax.dot_general(left, right, (dims, ((), ())), preferred_element_type=F32)


def dot_last(left, right):
    return dot(left, right, ((1,), (1,)))


def dot_first(left, right):
    return dot(left, right, ((0,), (0,)))


def bits_of(count):
    out = []
    bit = 1
    while bit < count:
        out.append(bit)
        bit *= 2
    return out


class Blocks:
    def __init__(self, refs):
        self.refs = refs

    def at(self, mask):
        return self.refs[mask][...]

    def put(self, mask, value):
        self.refs[mask][...] = value


def taker(refs):
    rest = list(refs)

    def take(count=None):
        got = [rest.pop(0) for _ in range(1 if count is None else count)]
        return got[0] if count is None else Blocks(got)

    return take


class Rows:
    def __init__(self, ref, at):
        self.ref, self.at = ref, at
        self.rows = ref.shape[2]

    def get(self, which, mask, width):
        start = (self.at[0] ^ mask) * width
        block = start // self.rows
        where = pl.ds(pl.multiple_of(start - block * self.rows, width), width)
        return self.ref[self.at[1] ^ block, which, where, :]


def span(col, mask, width):
    return pl.ds(pl.multiple_of((col ^ mask) * width, width), width)


GAIN_ONE, SHIFT_ONE, GAIN_TWO, SHIFT_TWO, BIAS_PROJ, SCALE_ONE, SCALE_TWO = range(7)


def vec_at(vecs, mask, which):
    return vecs.refs[mask][which : which + 1, :]


def norm_all(blocks, model):
    mean = sum(jnp.sum(b, axis=1, keepdims=True) for b in blocks) / model
    var = sum(jnp.sum(b * b, axis=1, keepdims=True) for b in blocks) / model - mean * mean
    inv = lax.rsqrt(var + EPS)
    return [(b - mean) * inv for b in blocks], inv


def probs_of(q, k, bias):
    scores = dot_last(q, k) * (HEAD_DIM ** (-0.5)) + bias
    top = jnp.max(scores, axis=-1, keepdims=True)
    raised = jnp.exp(scores - top)
    return raised * (1.0 / jnp.sum(raised, axis=-1, keepdims=True))


def over_heads(count, one):
    group = 2 if count % 2 == 0 else count
    lanes = group * HEAD_DIM

    def step(p, _):
        one(p * group, group, pl.ds(pl.multiple_of(p * lanes, lanes), lanes))
        return 0

    lax.fori_loop(0, count // group, step, 0)


def front_kernel(n, at, *refs):
    col, take = at[0], taker(refs)
    x, vecs = take(n), take(n)
    w_attn, qkv_bias, bias, norm_o, qkv_o, attn_o = (take() for _ in range(6))
    out = take(n)
    weights_of = Rows(w_attn, at)
    width = x.refs[0].shape[1]
    hats, _ = norm_all([x.at(m).astype(F32) for m in range(n)], n * width)
    sums = [None] * 3
    for m in range(n):
        rows = span(col, m, width)
        norm = (hats[m] * vec_at(vecs, m, GAIN_ONE) + vec_at(vecs, m, SHIFT_ONE)).astype(BF)
        norm_o[:, rows] = norm
        for j in range(3):
            term = dot(norm, weights_of.get(j, m, width))
            sums[j] = term if m == 0 else sums[j] + term
    qkv = [
        (sums[0] + qkv_bias[0:1]).astype(BF),
        sums[1].astype(BF),
        (sums[2] + qkv_bias[1:2]).astype(BF),
    ]
    for j in range(3):
        qkv_o[j] = qkv[j]

    def attend(first, group, lanes):
        q, k, v = (qkv_o[j, :, lanes] for j in range(3))
        outs = []
        for i in range(group):
            part = slice(i * HEAD_DIM, (i + 1) * HEAD_DIM)
            weights = probs_of(q[:, part], k[:, part], bias[first + i].astype(F32))
            outs.append(dot(weights.astype(BF), v[:, part]))
        attn_o[:, lanes] = jnp.concatenate(outs, axis=1).astype(BF)

    over_heads(bias.shape[0], attend)
    attn = attn_o[...]
    for m in range(n):
        out.put(m, dot_last(attn, weights_of.get(3, m, width)).astype(BF))


def middle_kernel(n, g, at, *refs):
    col, take = at[0], taker(refs)
    x, p, gm, vecs = (take(n) for _ in range(4))
    w_fc, fc1_bias, hat_o, inv_o, norm_o, gmlp_o, act_o, pre_o, sum_o = (take() for _ in range(9))
    out = take(n)
    weights_of = Rows(w_fc, at)
    width = x.refs[0].shape[1]
    mids = [
        x.at(m).astype(F32)
        + vec_at(vecs, m, SCALE_ONE) * (p.at(m).astype(F32) + vec_at(vecs, m, BIAS_PROJ))
        for m in range(n)
    ]
    hats, inv = norm_all(mids, n * width)
    inv_o[...] = jnp.broadcast_to(inv, inv_o.shape)
    pre, grad_act = None, None
    for m in range(n):
        rows = span(col, m, width)
        hat_o[m] = hats[m].astype(BF)
        norm = (hats[m] * vec_at(vecs, m, GAIN_TWO) + vec_at(vecs, m, SHIFT_TWO)).astype(BF)
        norm_o[:, rows] = norm
        grad_mlp = gm.refs[m][g]
        gmlp_o[:, rows] = grad_mlp
        one, two = dot(norm, weights_of.get(0, m, width)), dot(grad_mlp, weights_of.get(1, m, width))
        pre, grad_act = (one, two) if m == 0 else (pre + one, grad_act + two)
    pre = pre + fc1_bias[...]
    gate = 0.5 * (1.0 + lax.erf(pre * SQRT_HALF))
    act_o[...] = (pre * gate).astype(BF)
    slope = gate + pre * jnp.exp(-0.5 * pre * pre) * INV_ROOT_TWO_PI
    grad_pre = (grad_act * slope).astype(BF)
    pre_o[...] = grad_pre
    sum_o[...] = jnp.sum(grad_pre.astype(F32), axis=0, keepdims=True)
    for m in range(n):
        out.put(m, dot_last(grad_pre, weights_of.get(0, m, width)).astype(BF))


def mlp_kernel(n, at, *refs):
    take = taker(refs)
    act_a, act_b, w_fc = take(), take(), take()
    out = take(n)
    weights_of = Rows(w_fc, at)
    width = out.refs[0].shape[2]
    for m in range(n):
        rows = weights_of.get(1, m, width)
        for j, act in enumerate((act_a, act_b)):
            out.refs[m][j] = dot_last(act[...], rows).astype(BF)


def back_kernel(n, g, at, *refs):
    col, take = at[0], taker(refs)
    d_two = take(n)
    hat_two, inv_two = take(), take()
    gm, p_own, vecs = take(n), take(), take(n)
    qkv, bias, w_attn = (take() for _ in range(3))
    x = take(n)
    before = [take() for _ in range(min(g, 1))]
    attn_in_o, mid_o, dqkv_o, sum_o, total_o = (take() for _ in range(5))
    out = take(n)
    weights_of = Rows(w_attn, at)
    width = x.refs[0].shape[1]
    model = n * width
    scale = HEAD_DIM ** (-0.5)
    inv = inv_two[:, 0:1]
    scaled = [d_two.at(m).astype(F32) * vec_at(vecs, m, GAIN_TWO) for m in range(n)]
    hats = [hat_two[m].astype(F32) for m in range(n)]
    mean_one = sum(jnp.sum(s, axis=1, keepdims=True) for s in scaled) / model
    mean_two = sum(jnp.sum(s * h, axis=1, keepdims=True) for s, h in zip(scaled, hats)) / model
    grad_heads = None
    for m in range(n):
        rows = span(col, m, width)
        mid = gm.refs[m][g].astype(F32) / vec_at(vecs, m, SCALE_TWO) + inv * (
            scaled[m] - mean_one - hats[m] * mean_two
        )
        biased = mid * vec_at(vecs, m, SCALE_ONE)
        attn_in = biased.astype(BF)
        attn_in_o[:, rows] = attn_in
        term = dot(attn_in, weights_of.get(3, m, width))
        grad_heads = term if m == 0 else grad_heads + term
        if m == 0:
            mid_o[...] = mid
            d_own = d_two.at(0).astype(F32)
            proj_val = p_own[...].astype(F32) + vec_at(vecs, 0, BIAS_PROJ)
            for place, value in ((2, biased), (3, mid * proj_val), (4, d_own * hats[0]), (5, d_own)):
                sum_o[place : place + 1, :] = jnp.sum(value, axis=0, keepdims=True)
    dqkv_o[0] = grad_heads.astype(BF)

    def attend_back(first, group, lanes):
        q_all, k_all, v_all = (qkv[j, :, lanes] for j in range(3))
        d_all = dqkv_o[0, :, lanes]
        parts = [[], [], []]
        for i in range(group):
            part = slice(i * HEAD_DIM, (i + 1) * HEAD_DIM)
            q, k, v, d_out = (a[:, part] for a in (q_all, k_all, v_all, d_all))
            prob = probs_of(q, k, bias[first + i].astype(F32))
            grad_p = dot_last(d_out, v)
            row_dot = jnp.sum(prob * grad_p, axis=-1, keepdims=True)
            grad_s = (prob * (grad_p - row_dot)).astype(BF)
            parts[0].append(dot(grad_s, k) * scale)
            parts[1].append(dot_first(grad_s, q) * scale)
            parts[2].append(dot_first(prob.astype(BF), d_out))
        for j in range(3):
            dqkv_o[j, :, lanes] = jnp.concatenate(parts[j], axis=1).astype(BF)

    over_heads(bias.shape[0], attend_back)
    grads = [dqkv_o[j] for j in range(3)]
    for place, j in ((0, 0), (1, 2)):
        sum_o[place : place + 1, :] = jnp.sum(grads[j].astype(F32), axis=0, keepdims=True)
    sum_o[6:8, :] = jnp.zeros((2, width), F32)
    hats, _ = norm_all([x.at(m).astype(F32) for m in range(n)], model)
    total_one, total_two = 0.0, 0.0
    for m in range(n):
        full = sum(dot_last(grads[j], weights_of.get(j, m, width)) for j in range(3))
        out.put(m, full.astype(BF))
        hatted = full * hats[m]
        gain = vec_at(vecs, m, GAIN_ONE)
        total_one = total_one + jnp.sum(full * gain, axis=1, keepdims=True)
        total_two = total_two + jnp.sum(hatted * gain, axis=1, keepdims=True)
    shape = (total_one.shape[0], 128)
    pair = jnp.where(lax.broadcasted_iota(jnp.int32, shape, 1) == 0, total_one, total_two)
    pick = lax.broadcasted_iota(jnp.int32, (8, 128), 0) == lax.broadcasted_iota(jnp.int32, (8, 128), 1)
    for ref in before:
        total_o[0 : 8 * g, :] = ref[...]
    total_o[8 * g : 8 * g + 8, :] = lax.dot_general(
        pick.astype(F32),
        pair,
        (((1,), (1,)), ((), ())),
        precision=lax.Precision.HIGHEST,
        preferred_element_type=F32,
    )


def weight_kernel(n, pairs, members, at, *refs):
    row = at[1]
    left_a, left_b, right_a, right_b = (refs[i * pairs : (i + 1) * pairs] for i in range(4))
    out = Blocks(refs[4 * pairs :])
    rows = out.refs[0].shape[1]
    for m in range(n):
        where = span(row, m, rows)
        for j, member in enumerate(members):
            pick = lambda ref: ref[...] if member is None else ref[member]
            out.refs[m][j] = (
                dot_first(left_a[j][:, where], pick(right_a[j]))
                + dot_first(left_b[j][:, where], pick(right_b[j]))
            ).astype(BF)


class Near:
    def __init__(self, value):
        self.value = value


def kernel_call(body, outs, at, *args):
    def placed(a):
        return a.value if isinstance(a, Near) else pltpu.with_memory_space_constraint(a, pltpu.HBM)

    return pl.pallas_call(
        body,
        out_shape=[pltpu.HBM(*o) for o in outs],
        in_specs=[pl.BlockSpec(memory_space=pltpu.SMEM)] + [pl.BlockSpec()] * len(args),
        out_specs=[pl.BlockSpec()] * len(outs),
        compiler_params=pltpu.CompilerParams(vmem_limit_bytes=40 * 2**20),
    )(at, *[placed(a) for a in args])


def make_body(n_img, n_row, n_col):
    sizes = {"img": n_img, "row": n_row, "col": n_col}

    def swap(value, axis, mask):
        return lax.ppermute(value, axis, [(i, i ^ mask) for i in range(sizes[axis])])

    def gather_blocks(value, axis="col"):
        pieces = [value] * sizes[axis]
        for m in range(1, sizes[axis]):
            low = m & -m
            pieces[m] = swap(pieces[m ^ low], axis, low)
        return pieces

    def scatter_blocks(blocks, axis):
        held = [[block] for block in blocks]
        for m in scatter_order(sizes[axis]):
            low = m & -m
            send = held[m][0]
            if len(held[m]) > 1:
                send = sum(h.astype(F32) for h in held[m]).astype(send.dtype)
            held[m ^ low].append(swap(send, axis, low))
        return sum(h.astype(F32) for h in held[0])

    def all_sum(value, axes):
        for axis in axes:
            for bit in bits_of(sizes[axis]):
                value = value + swap(value, axis, bit)
        return value

    def gather_rows(values):
        return jnp.stack(gather_blocks(jnp.stack(values, axis=0), "row"), axis=0)

    def reduce_weights(blocks):
        share = scatter_blocks(blocks, "row").astype(BF)
        img_bits = bits_of(n_img)
        for bit in img_bits[:-1]:
            share = share.astype(F32) + swap(share, "img", bit).astype(F32)
            share = share.astype(BF)
        got = swap(share, "img", img_bits[-1])
        return [share[k].astype(F32) + got[k].astype(F32) for k in range(share.shape[0])]

    def body(
        tokens,
        attn_bias,
        first_gain,
        first_shift,
        qkv_weight,
        qkv_bias,
        proj_weight,
        proj_bias,
        scale_attn,
        second_gain,
        second_shift,
        fc1_weight,
        fc1_bias,
        fc2_weight,
        fc2_bias,
        scale_mlp,
        cotangent,
    ):
        count_rows, width = tokens.shape
        images = range(count_rows // SEQ)
        model = width * n_col
        hidden = fc1_weight.shape[1]
        at = jnp.stack([lax.axis_index("col"), lax.axis_index("row")]).astype(jnp.int32)

        def padded(value, g):
            return jnp.pad(value[g * SEQ : (g + 1) * SEQ], ((0, ROWS - SEQ), (0, 0)))

        x_own = [padded(tokens, g) for g in images]
        x_got = [gather_blocks(x_own[g]) for g in images]
        vectors = jnp.stack(
            [
                first_gain,
                first_shift,
                second_gain,
                second_shift,
                proj_bias,
                scale_attn,
                scale_mlp,
                scale_mlp,
            ],
            axis=0,
        )
        vecs = gather_blocks(vectors)
        w_attn = gather_rows([qkv_weight[:, 0], qkv_weight[:, 1], qkv_weight[:, 2], proj_weight])
        late_cot, _ = lax.optimization_barrier((cotangent, x_got[0][1]))
        gm_own = (late_cot * scale_mlp).astype(BF)
        gm_got = gather_blocks(jnp.stack([padded(gm_own, g) for g in images]))
        w_fc = gather_rows([fc1_weight, fc2_weight])
        bias = jnp.pad(attn_bias, ((0, 0), (0, 0), (0, ROWS - SEQ)), constant_values=MASKED)
        bias = jnp.pad(bias, ((0, 0), (0, ROWS - SEQ), (0, 0)))

        blocks = [((ROWS, width), BF)] * n_col
        wide = ((ROWS, model), BF)
        front, p_sum, p_got = [], [], []
        for g in images:
            front.append(
                kernel_call(
                    functools.partial(front_kernel, n_col),
                    [wide, ((3, ROWS, width), BF), ((ROWS, width), BF), *blocks],
                    at, *x_got[g], *vecs, Near(w_attn), qkv_bias, Near(bias),
                )
            )
            p_sum.append(scatter_blocks(front[g][3:], "col"))
            p_got.append(gather_blocks(p_sum[g].astype(BF)))

        middle, d_sum, d_got = [], [], []
        for g in images:
            middle.append(
                kernel_call(
                    functools.partial(middle_kernel, n_col, g),
                    [
                        ((n_col, ROWS, width), BF), ((ROWS, 128), F32), wide, wide,
                        ((ROWS, hidden), BF), ((ROWS, hidden), BF), ((1, hidden), F32), *blocks,
                    ],
                    at, *x_got[g], *p_got[g], *gm_got, *vecs, Near(w_fc), fc1_bias[None],
                )
            )
            d_sum.append(scatter_blocks(middle[g][7:], "col"))
            d_got.append(gather_blocks(d_sum[g].astype(BF)))

        def weight_grads(lefts, rights, members):
            rows, cols = lefts[0][0].shape[1] // n_row, rights[0][0].shape[-1]
            parts = kernel_call(
                functools.partial(weight_kernel, n_row, len(lefts), members),
                [((len(lefts), rows, cols), BF)] * n_row,
                at,
                *[t[g] for g in images for t in lefts],
                *[t[g] for g in images for t in rights],
            )
            return reduce_weights(parts)

        each = lambda results, k: [results[g][k] for g in images]
        grad_fc1 = weight_grads([each(middle, 2)], [each(middle, 5)], [None])
        grad_fc2 = weight_grads([each(middle, 3)], [each(middle, 4)], [None])
        mlp_blocks = kernel_call(
            functools.partial(mlp_kernel, n_col),
            [((2, ROWS, width), BF)] * n_col,
            at, middle[0][4], middle[1][4], Near(w_fc),
        )

        back = []
        for g in images:
            back.append(
                kernel_call(
                    functools.partial(back_kernel, n_col, g),
                    [
                        wide, ((ROWS, width), F32), ((3, ROWS, width), BF), ((8, width), F32),
                        ((8 * g + 8, ROWS), F32), *blocks,
                    ],
                    at, *d_got[g], middle[g][0], middle[g][1], *gm_got, p_got[g][0], *vecs,
                    front[g][1], Near(bias), Near(w_attn), *x_got[g], *[b[4] for b in back[g - 1 : g]],
                )
            )
        grad_one = [scatter_blocks(back[g][5:], "col") for g in images]
        totals = back[-1][4]
        totals = all_sum(totals, ("col",)) / model

        d_qkv = each(back, 2)
        grad_qk = weight_grads([each(front, 0)] * 2, [d_qkv, d_qkv], [0, 1])
        grad_vp = weight_grads([each(front, 0), each(back, 0)], [d_qkv, each(front, 2)], [2, None])
        grad_qkv = jnp.stack([*grad_qk, grad_vp[0]], axis=0)
        mlp_sum = scatter_blocks(mlp_blocks, "col")

        join = lambda a: jnp.concatenate([v[:SEQ] for v in a], axis=0)
        mlp_val = join([mlp_sum[g] for g in images]) + fc2_bias
        x_val = tokens.astype(F32)
        out_y = x_val + scale_attn * (join(p_sum) + proj_bias) + scale_mlp * mlp_val

        grad_tokens, one_sums = [], []
        for g in images:
            hats, inv = norm_all([b.astype(F32) for b in x_got[g]], model)
            hat = hats[0]
            one_sums.append(jnp.stack([jnp.sum(grad_one[g] * hat, axis=0), jnp.sum(grad_one[g], axis=0)]))
            grad_tokens.append(
                back[g][1]
                + inv
                * (grad_one[g] * first_gain - totals[8 * g][:, None] - hat * totals[8 * g + 1][:, None])
            )

        last_cot, _ = lax.optimization_barrier((cotangent, back[0][3]))
        cot_sums = [jnp.sum(last_cot, axis=0) * scale_mlp, jnp.sum(last_cot * mlp_val, axis=0)]
        own = jnp.concatenate(
            [
                back[0][3][:6] + back[1][3][:6],
                jnp.stack(cot_sums),
                one_sums[0] + one_sums[1],
                (middle[0][6] + middle[1][6]).reshape(-1, width),
            ],
            axis=0,
        )
        own = all_sum(own, ("row", "img"))
        sum_pre = own[10:].reshape(-1)
        return (
            out_y,
            join(grad_tokens),
            jnp.transpose(grad_qkv, (1, 0, 2)),
            own[0:2],
            grad_vp[1],
            own[2],
            own[3],
            grad_fc1[0],
            sum_pre,
            grad_fc2[0],
            own[6],
            own[7],
            own[8],
            own[9],
            own[4],
            own[5],
        )

    return body


def scatter_order(count):
    return sorted(range(1, count), key=lambda m: (m & -m, -m))


def solution(mesh):
    counts = (mesh.shape["img"], mesh.shape["row"], mesh.shape["col"])
    step = sharded(mesh, make_body(*counts))
    return step


def sharded(mesh, body):
    return jax.shard_map(
        body,
        mesh=mesh,
        in_specs=(
            P(("img", "row"), "col"),
            P("col", None, None),
            P("col"),
            P("col"),
            P("row", None, "col"),
            P(None, "col"),
            P("row", "col"),
            P("col"),
            P("col"),
            P("col"),
            P("col"),
            P("row", "col"),
            P("col"),
            P("row", "col"),
            P("col"),
            P("col"),
            P(("img", "row"), "col"),
        ),
        out_specs=(
            P(("img", "row"), "col"),
            P(("img", "row"), "col"),
            P("row", None, "col"),
            P(None, "col"),
            P("row", "col"),
            P("col"),
            P("col"),
            P("row", "col"),
            P("col"),
            P("row", "col"),
            P("col"),
            P("col"),
            P("col"),
            P("col"),
            P("col"),
            P("col"),
        ),
        check_vma=False,
    )
```
